512 devices in a mesh: patch: 64 (over z, y), field: 8 (over x, core).
Axes of the slice: x: 4, y: 8, z: 8, core: 2. Of those that a mesh axis runs over, the one named last changes fastest.
Arguments:
- pressure_start: float32 [512, 32, 1024], P('patch', 'field'), may hold values from -6 to 6
- divergence: float32 [512, 32, 1024], P('patch', 'field'), may hold values from -6 to 6
- neighbors: int32 [512, 6], P('patch'), may hold values from -1 to 511, as said below
- advect_slot: int32 [512], P('patch'), may hold values from 0 to 63, as said below
- point_cell: int32 [8192], replicated, may hold values from 0 to 16777215
- point_force: float32 [8192], P(('patch', 'field')), may hold values from -24 to 24
Outputs:
- remapped: bfloat16 [4096, 3, 32, 1024], P('patch', None, 'field')
The draws below stay inside these ranges and needn't reach their ends.
Inputs may be any that keep to these rules, and one draw needn't show every extreme that they name: `neighbors`: the low x neighbour of a patch held by index i of patch is held by index i - 1 and the high x neighbour by index i + 1, -1 where the domain ends in x; the y and z neighbours are held by the same index of patch as the patch. `advect_slot`: the 8 patches of one index of patch all have different entries; one owner, the same for every source, receives one patch from every index of patch.
All inputs are finite; a program needn't handle non-finite values.
Results may differ from the reference program's by a relative error of at most 0.0045.
Values may be sent and summed in bfloat16 or wider, within the bound.
A program may use at most 64 MiB of HBM per device.

```python
import jax
import jax.numpy as jnp

SIDE = 32
PPD = 8
SWEEPS = 6
PATCHES = 512
CAP = 1
SLOTS = 4096
POINTS = 8192
N_PATCH = 64


def draw_neighbors(key, part):
    key_list = jax.random.split(jax.random.fold_in(key, 11), N_PATCH)
    slot_order = jax.vmap(lambda sub_key: jax.random.permutation(sub_key, PPD))(key_list).astype(jnp.int32)
    layer_index = jnp.arange(N_PATCH, dtype=jnp.int32)[:, None]
    position = jnp.arange(PPD, dtype=jnp.int32)[None, :]
    row_length = PPD // 4
    y_place = position // row_length
    z_place = position % row_length
    patch_ids = layer_index * PPD + slot_order
    layer_full = jnp.broadcast_to(layer_index, (N_PATCH, PPD))
    position_full = jnp.broadcast_to(position, (N_PATCH, PPD))
    lower_layer = jnp.clip(layer_full - 1, 0, N_PATCH - 1)
    upper_layer = jnp.clip(layer_full + 1, 0, N_PATCH - 1)
    x_low = jnp.where(layer_full > 0, patch_ids[lower_layer, position_full], -1)
    x_high = jnp.where(layer_full < N_PATCH - 1, patch_ids[upper_layer, position_full], -1)
    y_low = patch_ids[layer_full, jnp.broadcast_to((y_place - 1) % 4 * row_length + z_place, (N_PATCH, PPD))]
    y_high = patch_ids[layer_full, jnp.broadcast_to((y_place + 1) % 4 * row_length + z_place, (N_PATCH, PPD))]
    z_low = patch_ids[layer_full, jnp.broadcast_to(y_place * row_length + (z_place - 1) % row_length, (N_PATCH, PPD))]
    z_high = patch_ids[layer_full, jnp.broadcast_to(y_place * row_length + (z_place + 1) % row_length, (N_PATCH, PPD))]
    link_rows = jnp.stack([x_low, x_high, y_low, y_high, z_low, z_high], axis=-1).reshape(-1, 6)
    result = jnp.zeros((N_PATCH * PPD, 6), jnp.int32).at[patch_ids.reshape(-1)].set(link_rows.astype(jnp.int32))
    return result.astype(jnp.int32)


def draw_advect_slot(key, part):
    all_slots = N_PATCH * CAP
    busiest = jax.random.randint(jax.random.fold_in(key, 5), (), 0, N_PATCH)
    key_list = jax.random.split(jax.random.fold_in(key, 7), N_PATCH)

    def per_source(sub_key):
        key_first, key_second = jax.random.split(sub_key)
        slot_list = jax.random.permutation(key_first, all_slots).astype(jnp.int32)
        counter = jnp.arange(all_slots, dtype=jnp.int32)
        priority = jnp.where(slot_list // CAP == busiest, counter, all_slots + counter)
        chosen = slot_list[jnp.argsort(priority)][:PPD]
        return chosen[jax.random.permutation(key_second, PPD)]
    return jax.vmap(per_source)(key_list).reshape(-1).astype(jnp.int32)


def touch_ends(values, own_key, smallest, high):
    place = [jax.random.randint(jax.random.fold_in(own_key, axis), (), 0, length) for axis, length in enumerate(values.shape)]
    widest = values.shape.index(max(values.shape))
    neighbour = place[:widest] + [(place[widest] + 1) % values.shape[widest]] + place[widest + 1:]
    return values.at[tuple(place)].set(smallest).at[tuple(neighbour)].set(high)


def steps_of(rng, dims, cuts, low, top_value):
    level, own = 1.0, jax.random.fold_in(rng, 6)
    for dim, shards_of in cuts:
        steps = jnp.exp(jax.random.uniform(jax.random.fold_in(own, dim), (shards_of,), jnp.float32, low / len(cuts), top_value / len(cuts)))
        level = level * jnp.repeat(steps, dims[dim] // shards_of).reshape([-1 if axis == dim else 1 for axis in range(len(dims))])
    return level


def noise(key, dims, width, most, cuts=(), held_as=jnp.bfloat16):
    factor_of = steps_of(key, dims, cuts, -0.22, 0.18) if cuts else 1.0
    values = jax.random.normal(key, dims, jnp.float32) * width * factor_of
    return jnp.minimum(jnp.maximum(values, -most), most).astype(held_as)


def setup_inputs(seed: int = 0) -> dict:
    keys = jax.random.split(jax.random.key(seed), 7)
    pressure_start = noise(keys[0], (PATCHES, SIDE, SIDE * SIDE), 1.0, 6.0, ((0, 64), (1, 8)), jnp.float32)
    divergence = noise(keys[1], (PATCHES, SIDE, SIDE * SIDE), 1.0, 6.0, ((0, 64), (1, 8)), jnp.float32)
    neighbors = draw_neighbors(jax.random.fold_in(keys[6], 71), 0)
    advect_slot = draw_advect_slot(jax.random.fold_in(keys[6], 71), 0)
    point_cell = touch_ends(jax.random.randint(keys[4], (POINTS,), 0, PATCHES * SIDE * SIDE * SIDE), jax.random.fold_in(keys[4], 1), 0, (PATCHES * SIDE * SIDE * SIDE) - 1).astype(jnp.int32)
    point_force = noise(keys[5], (POINTS,), 4.0, 24.0, ((0, 512),), jnp.float32)
    return {"pressure_start": pressure_start, "divergence": divergence, "neighbors": neighbors, "advect_slot": advect_slot, "point_cell": point_cell, "point_force": point_force}


relaxation = 1.0 / 9.0


def side_faces(pressure, link_table):
    plane_area = pressure.shape[-1]
    south_face = pressure[:, :, plane_area - SIDE:][link_table[:, 2]]
    north_face = pressure[:, :, :SIDE][link_table[:, 3]]
    below_face = pressure[:, :, SIDE - 1::SIDE][link_table[:, 4]]
    above_face = pressure[:, :, 0::SIDE][link_table[:, 5]]
    return south_face, north_face, below_face, above_face


def stencil_values(pressure, west_plane, east_plane, side_rows):
    plane_area = pressure.shape[-1]
    cell_index = jnp.arange(plane_area, dtype=jnp.int32)
    y_index = cell_index // SIDE
    z_index = cell_index % SIDE
    south_face, north_face, below_face, above_face = side_rows
    to_west = jnp.concatenate([west_plane[:, None], pressure[:, :-1]], axis=1)
    to_east = jnp.concatenate([pressure[:, 1:], east_plane[:, None]], axis=1)
    to_south = jnp.where(y_index == 0, jnp.tile(south_face, (1, 1, SIDE)), jnp.roll(pressure, SIDE, axis=-1))
    to_north = jnp.where(y_index == SIDE - 1, jnp.tile(north_face, (1, 1, SIDE)), jnp.roll(pressure, -SIDE, axis=-1))
    to_below = jnp.where(z_index == 0, jnp.repeat(below_face, SIDE, axis=-1), jnp.roll(pressure, 1, axis=-1))
    to_above = jnp.where(z_index == SIDE - 1, jnp.repeat(above_face, SIDE, axis=-1), jnp.roll(pressure, -1, axis=-1))
    return to_west, to_east, to_south, to_north, to_below, to_above


def sweep(pressure, source, values):
    to_west, to_east, to_south, to_north, to_below, to_above = values
    neighbor_sum = to_west + to_east + to_south + to_north + to_below + to_above
    return pressure + relaxation * (source - (6.0 * pressure - neighbor_sum))


def gradient(values):
    to_west, to_east, to_south, to_north, to_below, to_above = values
    stacked = jnp.stack([0.5 * (to_east - to_west), 0.5 * (to_north - to_south), 0.5 * (to_above - to_below)], axis=1)
    return stacked.astype(jnp.bfloat16)


def reference(pressure_start, divergence, neighbors, advect_slot, point_cell, point_force):
    source = divergence.reshape(-1).at[point_cell].add(point_force).reshape(divergence.shape)
    west_index = jnp.clip(neighbors[:, 0], 0, PATCHES - 1)
    east_index = jnp.clip(neighbors[:, 1], 0, PATCHES - 1)
    west_valid = (neighbors[:, 0] >= 0)[:, None]
    east_valid = (neighbors[:, 1] >= 0)[:, None]

    def ghost_planes(pressure):
        west_plane = jnp.where(west_valid, pressure[west_index, SIDE - 1], 0.0)
        east_plane = jnp.where(east_valid, pressure[east_index, 0], 0.0)
        return west_plane, east_plane

    pressure = pressure_start
    for sweep_step in range(SWEEPS):
        west_plane, east_plane = ghost_planes(pressure)
        values = stencil_values(pressure, west_plane, east_plane, side_faces(pressure, neighbors))
        pressure = sweep(pressure, source, values)
    west_plane, east_plane = ghost_planes(pressure)
    gradients = gradient(stencil_values(pressure, west_plane, east_plane, side_faces(pressure, neighbors)))
    source_index = jnp.arange(PATCHES, dtype=jnp.int32) // PPD
    destination = advect_slot // CAP
    within = advect_slot % CAP
    where_to = (destination * N_PATCH + source_index) * CAP + within
    remapped = jnp.zeros((SLOTS, 3, SIDE, SIDE * SIDE), jnp.bfloat16).at[where_to].set(gradients)
    return remapped
```

```python
import functools
import math

import jax
import jax.numpy as jnp
from jax import lax
from jax.experimental import pallas as pl
from jax.experimental.pallas import tpu as pltpu
from jax.sharding import PartitionSpec as P

SIDE = 32
SWEEPS = 6
PPD = 8
PLANES = 4
AREA = SIDE * SIDE
CHUNKS = AREA // 128
SLABS = 5
LANES = 128
REGION = 16
ROWS_HOT = REGION * PPD * (AREA // 256)
MESH = pl.DeviceIdType.MESH

relaxation = 1.0 / 9.0


def lane_iota():
    return lax.broadcasted_iota(jnp.int32, (PPD, LANES), 1)


def by_patch(value, index):
    return jnp.take_along_axis(value, index, axis=0, mode="promise_in_bounds")


def by_lane(value, index):
    return jnp.take_along_axis(value, index, axis=1, mode="promise_in_bounds")


def side_values(center, idx_south, idx_north, idx_z):
    lane = lane_iota()
    z = lane % SIDE
    up = [pltpu.roll(c, SIDE, 1) for c in center]
    down = [pltpu.roll(c, LANES - SIDE, 1) for c in center]
    first = by_patch(up[CHUNKS - 1], idx_south)
    last = by_patch(down[0], idx_north)
    south, north, below, above, faces = [], [], [], [], []
    for v in range(CHUNKS):
        south.append(jnp.where(lane < SIDE, first if v == 0 else up[v - 1], up[v]))
        north.append(
            jnp.where(lane >= LANES - SIDE, last if v == CHUNKS - 1 else down[v + 1], down[v])
        )
        swapped = jnp.where(
            z == 0,
            pltpu.roll(center[v], LANES - (SIDE - 1), 1),
            pltpu.roll(center[v], SIDE - 1, 1),
        )
        face = by_patch(swapped, idx_z)
        faces.append(face)
        below.append(jnp.where(z == 0, face, pltpu.roll(center[v], 1, 1)))
        above.append(jnp.where(z == SIDE - 1, face, pltpu.roll(center[v], LANES - 1, 1)))
    return south, north, below, above, faces


def chunks_of(ref, k, row):
    return [ref[k, row, :, v * LANES : (v + 1) * LANES] for v in range(CHUNKS)]


def step_kernel(
    nz,
    ny,
    nf,
    inv_ref,
    p_ref,
    d_ref,
    tab_ref,
    frow_ref,
    pc_ref,
    out_ref,
    pa,
    pb,
    src,
    tabs,
    xbuf,
    ybuf,
    forces,
    hot_a,
    hot_b,
    scaled,
    acc,
    idx,
    packed,
    sbuf,
    load_sem,
    halo_send,
    halo_recv,
    x_send,
    x_recv,
    y_send,
    y_recv,
    z_send,
    z_recv,
    a_send,
    a_recv,
    own_sem,
):
    patch = lax.axis_index("patch")
    field = lax.axis_index("field")
    z_me = lax.div(patch, ny)
    y_me = lax.rem(patch, ny)
    total = nz * ny * nf
    line = patch * nf + field
    x_side = PLANES * nf

    def along_line(k):
        other = lax.rem(line + (k + total), total)
        return (lax.div(other, nf), lax.rem(other, nf))

    def along_x(k):
        return (patch, lax.rem(field + k, nf))

    def along_y(k):
        return (z_me * ny + lax.rem(y_me + k, ny), field)

    def along_z(k):
        return (lax.rem(z_me + k, nz) * ny + y_me, field)

    loads = []
    for x in range(PLANES):
        loads.append(
            pltpu.make_async_copy(p_ref.at[:, x, :], pa.at[2, x + 1], load_sem.at[0, x])
        )
        loads.append(pltpu.make_async_copy(d_ref.at[:, x, :], src.at[2, x], load_sem.at[1, x]))
    loads.append(pltpu.make_async_copy(tab_ref, tabs.at[2], load_sem.at[0, PLANES]))
    for copy in loads:
        copy.start()

    barrier = pltpu.get_barrier_semaphore()
    greeted = [along_x(k) for k in range(1, nf)]
    greeted += [along_y(k) for k in range(1, ny)]
    greeted += [along_z(k) for k in range(1, nz)]
    greeted += [along_line(k) for k in (1, -1, 2, -2)]
    for device in greeted:
        pl.semaphore_signal(barrier, inc=1, device_id=device, device_id_type=MESH)

    def build_hot(row, carry):
        zrow = lax.div(row, ny)
        yrow = lax.rem(row, ny)
        cell = pc_ref[pl.ds(row, 1), :]
        q = cell // (x_side * AREA)
        inside = cell % (x_side * AREA)
        plane = lax.div(q, PPD) * x_side + lax.div(inside, AREA)
        lp = lax.rem(q, PPD)
        cell_in_plane = lax.rem(inside, AREA)
        e = plane - (line * PLANES - 6)
        m = (lax.div(cell_in_plane, 256) * REGION + e) * PPD + lp
        m = jnp.where((e >= 0) & (e < REGION), m, -1)
        n = lax.rem(cell_in_plane, 256)
        lanes = pl.ds(pl.multiple_of(yrow * LANES, LANES), LANES)
        rows = lax.broadcasted_iota(jnp.int32, (ROWS_HOT, LANES), 0)
        hot_a[zrow, :, lanes] = jnp.where(rows == m, 1.0, 0.0).astype(jnp.bfloat16)
        columns = lax.broadcasted_iota(jnp.int32, (256, LANES), 0)
        hot_b[zrow, :, lanes] = jnp.where(columns == n, 1.0, 0.0).astype(jnp.bfloat16)
        return carry

    half = nz * ny // 2
    lax.fori_loop(0, half, build_hot, 0)
    for copy in loads:
        copy.wait()
    pl.semaphore_wait(barrier, len(greeted))

    def send(source, target, s_sem, r_sem, device):
        copy = pltpu.make_async_remote_copy(
            src_ref=source,
            dst_ref=target,
            send_sem=s_sem,
            recv_sem=r_sem,
            device_id=device,
            device_id_type=MESH,
        )
        copy.start()
        return copy

    x_copies = [
        send(frow_ref, xbuf.at[field], x_send.at[k - 1], x_recv.at[k - 1], along_x(k))
        for k in range(1, nf)
    ]
    halo = []
    for i, (k, lo, hi, dlo, dhi) in enumerate(
        ((1, 0, 4, 0, 4), (-1, 0, 4, 0, 4), (2, 1, 4, 2, 4), (-2, 0, 3, 0, 2))
    ):
        there = along_line(k)
        slot = 2 - k
        halo.append(
            send(
                pa.at[2, lo + 1 : hi + 1],
                pa.at[slot, lo + 1 : hi + 1],
                halo_send.at[0, i],
                halo_recv.at[0, i],
                there,
            )
        )
        halo.append(
            send(
                src.at[2, dlo:dhi],
                src.at[slot, dlo:dhi],
                halo_send.at[1, i],
                halo_recv.at[1, i],
                there,
            )
        )
        halo.append(
            send(tabs.at[2], tabs.at[slot], halo_send.at[2, i], halo_recv.at[2, i], there)
        )

    lax.fori_loop(half, nz * ny, build_hot, 0)

    for copy in x_copies:
        copy.wait_recv()
    row = frow_ref[...]
    for k in range(1, nf):
        row = row + xbuf[lax.rem(field + k, nf)]
    ybuf[y_me] = row
    y_copies = [
        send(ybuf.at[y_me], ybuf.at[y_me], y_send.at[k - 1], y_recv.at[k - 1], along_y(k))
        for k in range(1, ny)
    ]
    acc[...] = jnp.zeros_like(acc)
    for copy in y_copies:
        copy.wait_recv()
    z_copies = [
        send(ybuf, forces.at[z_me], z_send.at[k - 1], z_recv.at[k - 1], along_z(k))
        for k in range(1, nz)
    ]
    forces[z_me] = ybuf[...]

    def add_points(zrow):
        for part in range(2):
            for yrow in range(ny):
                force = forces[zrow, yrow]
                high = force.astype(jnp.bfloat16)
                if part == 1:
                    high = (force - high.astype(jnp.float32)).astype(jnp.bfloat16)
                wide = jnp.broadcast_to(high.astype(jnp.float32), (16, LANES)).astype(jnp.bfloat16)
                for b in range(16):
                    scaled[b * 16 : (b + 1) * 16, yrow * LANES : (yrow + 1) * LANES] = (
                        hot_b[zrow, b * 16 : (b + 1) * 16, yrow * LANES : (yrow + 1) * LANES] * wide
                    )
            acc[...] += lax.dot_general(
                hot_a[zrow],
                scaled[...],
                (((1,), (1,)), ((), ())),
                preferred_element_type=jnp.float32,
            )

    add_points(z_me)

    for copy in halo:
        copy.wait_recv()
    zero_idx = jnp.zeros((PPD, LANES), jnp.int32)
    own_row = lax.broadcasted_iota(jnp.int32, (PPD, LANES), 0)
    z_lane = lane_iota() % SIDE
    for k in range(SLABS):
        table = tabs[k]
        columns = [zero_idx + table[:, c : c + 1] for c in range(6)]
        fk = lax.rem(field + (k - 2 + nf), nf)
        idx[k, 0] = jnp.where(fk == 0, columns[0], own_row)
        idx[k, 1] = jnp.where(fk == nf - 1, columns[1], own_row)
        idx[k, 2] = columns[2] & (PPD - 1)
        idx[k, 3] = columns[3] & (PPD - 1)
        idx[k, 4] = jnp.where(z_lane == 0, columns[4], columns[5]) & (PPD - 1)

    def fill_ghosts(ref, edges):
        for k in edges:
            west, east = idx[k, 0], idx[k - 1, 1]
            west_values = chunks_of(ref, k - 1, PLANES)
            east_values = chunks_of(ref, k, 1)
            for v in range(CHUNKS):
                lanes = slice(v * LANES, (v + 1) * LANES)
                ref[k, 0, :, lanes] = jnp.where(
                    west >= 0, by_patch(west_values[v], west & (PPD - 1)), 0.0
                )
                ref[k - 1, PLANES + 1, :, lanes] = jnp.where(
                    east >= 0, by_patch(east_values[v], east & (PPD - 1)), 0.0
                )

    def sweep(old, new, lo, hi):
        def body(g, carry):
            k = lax.div(g, PLANES)
            j = lax.rem(g, PLANES)
            west = chunks_of(old, k, j)
            center = chunks_of(old, k, j + 1)
            east = chunks_of(old, k, j + 2)
            south, north, below, above, _ = side_values(center, idx[k, 2], idx[k, 3], idx[k, 4])
            for v in range(CHUNKS):
                around = west[v] + east[v] + south[v] + north[v] + below[v] + above[v]
                source = src[k, j, :, v * LANES : (v + 1) * LANES]
                new[k, j + 1, :, v * LANES : (v + 1) * LANES] = center[v] + relaxation * (
                    source - (6.0 * center[v] - around)
                )
            return carry

        lax.fori_loop(lo, hi + 1, body, 0)

    fill_ghosts(pa, range(1, SLABS))
    for copy in halo:
        copy.wait_send()
    sweep(pa, pb, 2, 17)

    for k in range(1, nz):
        z_copies[k - 1].wait_recv()
        add_points(lax.rem(z_me + (nz - k), nz))

    for e in range(REGION):
        k, j = divmod(e + 2, PLANES)
        for part in range(AREA // 256):
            extra = acc[(part * REGION + e) * PPD : (part * REGION + e + 1) * PPD, :]
            lanes = slice(part * 256, (part + 1) * 256)
            src[k, j, :, lanes] += extra
            pb[k, j + 1, :, lanes] += relaxation * extra

    refs = (pa, pb)
    for t in range(2, SWEEPS + 1):
        old, new = refs[(t + 1) % 2], refs[t % 2]
        reach = SWEEPS - t
        fill_ghosts(old, range(1, SLABS) if reach >= 1 else (2, 3))
        sweep(old, new, 7 - reach, 12 + reach)
    final = refs[SWEEPS % 2]
    fill_ghosts(final, (2, 3))

    values = [chunks_of(final, 2, r) for r in range(PLANES + 2)]
    level = values[1][0]
    for r in range(1, PLANES + 1):
        for v in range(CHUNKS):
            if (r, v) != (1, 0):
                level = level + values[r][v]
    level = jnp.sum(level, axis=1, keepdims=True) * (1.0 / (PLANES * AREA))
    lane = lane_iota()
    group = lane // SIDE
    within = lane % SIDE
    chunk_of_lane = within // 4
    face_lane = (within % 4) * SIDE + jnp.where(group == 2, SIDE - 1, 0)
    for r in range(PLANES + 2):
        for v in range(CHUNKS):
            packed[:PPD, r, v, :] = values[r][v] - level
    for r in range(1, PLANES + 1):
        south, north, _, _, faces = side_values(values[r], idx[2, 2], idx[2, 3], idx[2, 4])
        row = jnp.where(group == 0, south[0], north[CHUNKS - 1])
        for v in range(CHUNKS):
            use = (chunk_of_lane == v) & ((group == 1) | (group == 2))
            row = jnp.where(use, by_lane(faces[v], face_lane), row)
        packed[:PPD, PLANES + 2, r - 1, :] = row - level
        packed[:PPD, PLANES + 2, PLANES + r - 1, :] = jnp.zeros_like(row)
    packed[PPD] = jnp.zeros_like(packed[PPD])

    def fill_slot(d, carry):
        sbuf[d] = packed[inv_ref[d]].astype(jnp.bfloat16)
        return carry

    lax.fori_loop(0, nz * ny, fill_slot, 0)

    def remap_copy(i):
        a, b = lax.div(i, ny), lax.rem(i, ny)
        dz = lax.rem(a + b, nz)
        there = lax.rem(z_me + dz, nz) * ny + lax.rem(y_me + b, ny)
        return pltpu.make_async_remote_copy(
            src_ref=sbuf.at[there],
            dst_ref=out_ref.at[patch],
            send_sem=a_send.at[i],
            recv_sem=a_recv.at[i],
            device_id=(there, field),
            device_id_type=MESH,
        )

    def start_copy(i, carry):
        remap_copy(i).start()
        return carry

    def wait_copy(i, carry):
        remap_copy(i).wait()
        return carry

    own = pltpu.make_async_copy(sbuf.at[patch], out_ref.at[patch], own_sem)
    own.start()
    lax.fori_loop(1, nz * ny, start_copy, 0)
    for copy in x_copies + y_copies + z_copies:
        copy.wait_send()
    own.wait()
    lax.fori_loop(1, nz * ny, wait_copy, 0)


def gradient_kernel(in_ref, out_ref, turn):
    lane = lane_iota()
    chunk = lax.broadcasted_iota(jnp.int32, (CHUNKS, LANES), 0)
    z = lane % SIDE
    face_lane = jnp.where(z == 0, SIDE, 2 * SIDE) + chunk * 4 + lane // SIDE
    low_corner = (chunk == 0) & (lane < SIDE)
    high_corner = (chunk == CHUNKS - 1) & (lane >= LANES - SIDE)

    def body(s, carry):
        rows = [in_ref[s, r].astype(jnp.float32) for r in range(PLANES + 3)]
        for x in range(PLANES):
            center = rows[x + 1]
            face = jnp.broadcast_to(rows[PLANES + 2][x : x + 1, :], (CHUNKS, LANES))
            face_z = by_lane(face, face_lane)
            up = pltpu.roll(center, SIDE, 1)
            down = pltpu.roll(center, LANES - SIDE, 1)
            south = jnp.where(lane < SIDE, pltpu.roll(up, 1, 0), up)
            south = jnp.where(low_corner, face, south)
            north = jnp.where(lane >= LANES - SIDE, pltpu.roll(down, CHUNKS - 1, 0), down)
            north = jnp.where(high_corner, face, north)
            below = jnp.where(z == 0, face_z, pltpu.roll(center, 1, 1))
            above = jnp.where(z == SIDE - 1, face_z, pltpu.roll(center, LANES - 1, 1))
            turn[0, x] = 0.5 * (rows[x + 2] - rows[x])
            turn[1, x] = 0.5 * (north - south)
            turn[2, x] = 0.5 * (above - below)
        for c in range(3):
            for v in range(CHUNKS):
                out_ref[s, c, :, v * LANES : (v + 1) * LANES] = turn[c, :, v, :].astype(jnp.bfloat16)
        return carry

    lax.fori_loop(0, in_ref.shape[0], body, 0)


def on_device(pressure_start, divergence, neighbors, advect_slot, point_cell, point_force):
    n_patch = lax.axis_size("patch")
    nf = lax.axis_size("field")
    ny = math.isqrt(n_patch)
    nz = n_patch // ny
    field = lax.axis_index("field")
    per_device = point_force.shape[0]
    lane = jnp.arange(LANES, dtype=jnp.int32)
    spread = jnp.tile(point_force, LANES // per_device)
    frow = jnp.where(lane // per_device == field, spread, 0.0).reshape(1, LANES)
    table = jnp.pad(neighbors, ((0, 0), (0, LANES - 6)))
    cells = point_cell.reshape(n_patch, -1)
    if cells.shape[1] < LANES:
        cells = jnp.pad(cells, ((0, 0), (0, LANES - cells.shape[1])), constant_values=-1)
    owner = jnp.arange(n_patch, dtype=jnp.int32)
    order = jnp.arange(PPD, dtype=jnp.int32)
    hit = advect_slot[:, None] == owner[None, :]
    inverse = PPD - jnp.sum(jnp.where(hit, PPD - order[:, None], 0), axis=0, dtype=jnp.int32)

    anywhere = pl.BlockSpec(memory_space=pl.ANY)
    vmem = pl.BlockSpec(memory_space=pltpu.VMEM)
    dma = pltpu.SemaphoreType.DMA
    slot = (PLANES + 3, CHUNKS, LANES)
    received = pl.pallas_call(
        functools.partial(step_kernel, nz, ny, nf),
        out_shape=jax.ShapeDtypeStruct((n_patch,) + slot, jnp.bfloat16),
        in_specs=[
            pl.BlockSpec(memory_space=pltpu.SMEM),
            anywhere,
            anywhere,
            anywhere,
            vmem,
            vmem,
        ],
        out_specs=anywhere,
        scratch_shapes=[
            pltpu.VMEM((SLABS, PLANES + 2, PPD, AREA), jnp.float32),
            pltpu.VMEM((SLABS, PLANES + 2, PPD, AREA), jnp.float32),
            pltpu.VMEM((SLABS, PLANES, PPD, AREA), jnp.float32),
            pltpu.VMEM((SLABS, PPD, LANES), jnp.int32),
            pltpu.VMEM((nf, 1, LANES), jnp.float32),
            pltpu.VMEM((ny, 1, LANES), jnp.float32),
            pltpu.VMEM((nz, ny, 1, LANES), jnp.float32),
            pltpu.VMEM((nz, ROWS_HOT, ny * LANES), jnp.bfloat16),
            pltpu.VMEM((nz, 256, ny * LANES), jnp.bfloat16),
            pltpu.VMEM((256, ny * LANES), jnp.bfloat16),
            pltpu.VMEM((ROWS_HOT, 256), jnp.float32),
            pltpu.VMEM((SLABS, 5, PPD, LANES), jnp.int32),
            pltpu.VMEM((PPD + 1,) + slot, jnp.float32),
            pltpu.VMEM((n_patch,) + slot, jnp.bfloat16),
            dma((2, PLANES + 1)),
            dma((3, 4)),
            dma((3, 4)),
            dma((nf - 1,)),
            dma((nf - 1,)),
            dma((ny - 1,)),
            dma((ny - 1,)),
            dma((nz - 1,)),
            dma((nz - 1,)),
            dma((n_patch,)),
            dma((n_patch,)),
            dma,
        ],
        compiler_params=pltpu.CompilerParams(
            collective_id=0, has_side_effects=True, vmem_limit_bytes=48 * 1024 * 1024
        ),
        name="step",
    )(inverse, pressure_start, divergence, table, frow, cells)

    block = 8 if n_patch % 8 == 0 else n_patch
    return pl.pallas_call(
        gradient_kernel,
        grid=(n_patch // block,),
        out_shape=jax.ShapeDtypeStruct((n_patch, 3, PLANES, AREA), jnp.bfloat16),
        in_specs=[pl.BlockSpec((block,) + slot, lambda i: (i, 0, 0, 0))],
        out_specs=pl.BlockSpec((block, 3, PLANES, AREA), lambda i: (i, 0, 0, 0)),
        scratch_shapes=[pltpu.VMEM((3, PLANES, CHUNKS, LANES), jnp.float32)],
        name="gradient",
    )(received)


def solution(mesh):
    in_specs = (
        P("patch", "field", None),
        P("patch", "field", None),
        P("patch", None),
        P("patch"),
        P(),
        P(("patch", "field")),
    )
    out_specs = P("patch", None, "field", None)
    return jax.shard_map(
        on_device, mesh=mesh, in_specs=in_specs, out_specs=out_specs, check_vma=False
    )
```

```python
import functools
import math

import jax
import jax.numpy as jnp
from jax import lax
from jax.experimental import pallas as pl
from jax.experimental.pallas import tpu as pltpu
from jax.sharding import PartitionSpec as P

SIDE = 32
SWEEPS = 6
PPD = 8
PLANES = 4
AREA = SIDE * SIDE
CHUNKS = AREA // 128
SLABS = 5
LANES = 128
REGION = 16
ROWS_HOT = REGION * PPD * (AREA // 256)
MESH = pl.DeviceIdType.MESH

relaxation = 1.0 / 9.0


def lane_iota():
    return lax.broadcasted_iota(jnp.int32, (PPD, LANES), 1)


def by_patch(value, index):
    return jnp.take_along_axis(value, index, axis=0, mode="promise_in_bounds")


def by_lane(value, index):
    return jnp.take_along_axis(value, index, axis=1, mode="promise_in_bounds")


def side_values(center, idx_south, idx_north, idx_z):
    lane = lane_iota()
    z = lane % SIDE
    up = [pltpu.roll(c, SIDE, 1) for c in center]
    down = [pltpu.roll(c, LANES - SIDE, 1) for c in center]
    first = by_patch(up[CHUNKS - 1], idx_south)
    last = by_patch(down[0], idx_north)
    south, north, below, above, faces = [], [], [], [], []
    for v in range(CHUNKS):
        south.append(jnp.where(lane < SIDE, first if v == 0 else up[v - 1], up[v]))
        north.append(
            jnp.where(lane >= LANES - SIDE, last if v == CHUNKS - 1 else down[v + 1], down[v])
        )
        swapped = jnp.where(
            z == 0,
            pltpu.roll(center[v], LANES - (SIDE - 1), 1),
            pltpu.roll(center[v], SIDE - 1, 1),
        )
        face = by_patch(swapped, idx_z)
        faces.append(face)
        below.append(jnp.where(z == 0, face, pltpu.roll(center[v], 1, 1)))
        above.append(jnp.where(z == SIDE - 1, face, pltpu.roll(center[v], LANES - 1, 1)))
    return south, north, below, above, faces


def chunks_of(ref, k, row):
    return [ref[k, row, :, v * LANES : (v + 1) * LANES] for v in range(CHUNKS)]


def step_kernel(
    nz,
    ny,
    nf,
    adv_ref,
    force_ref,
    p_ref,
    d_ref,
    tab_ref,
    cell_ref,
    out_ref,
    inv_ref,
    frow_ref,
    pc_ref,
    rbuf,
    turn,
    stage,
    pa,
    pb,
    src,
    tabs,
    xbuf,
    ybuf,
    forces,
    hot_a,
    hot_b,
    scaled,
    acc,
    idx,
    packed,
    sbuf,
    load_sem,
    halo_send,
    halo_recv,
    x_send,
    x_recv,
    y_send,
    y_recv,
    z_send,
    z_recv,
    a_send,
    a_recv,
    out_sem,
):
    patch = lax.axis_index("patch")
    field = lax.axis_index("field")
    z_me = lax.div(patch, ny)
    y_me = lax.rem(patch, ny)
    total = nz * ny * nf
    line = patch * nf + field
    x_side = PLANES * nf

    def along_line(k):
        other = lax.rem(line + (k + total), total)
        return (lax.div(other, nf), lax.rem(other, nf))

    def along_x(k):
        return (patch, lax.rem(field + k, nf))

    def along_y(k):
        return (z_me * ny + lax.rem(y_me + k, ny), field)

    def along_z(k):
        return (lax.rem(z_me + k, nz) * ny + y_me, field)

    loads = []
    for x in range(PLANES):
        loads.append(
            pltpu.make_async_copy(p_ref.at[:, x, :], pa.at[2, x + 1], load_sem.at[0, x])
        )
        loads.append(pltpu.make_async_copy(d_ref.at[:, x, :], src.at[2, x], load_sem.at[1, x]))
    loads.append(pltpu.make_async_copy(tab_ref, tabs.at[2], load_sem.at[0, PLANES]))
    cells = pltpu.make_async_copy(cell_ref, pc_ref, load_sem.at[1, PLANES])
    cells.start()
    for copy in loads:
        copy.start()

    barrier = pltpu.get_barrier_semaphore()
    greeted = [along_x(k) for k in range(1, nf)]
    greeted += [along_y(k) for k in range(1, ny)]
    greeted += [along_z(k) for k in range(1, nz)]
    greeted += [along_line(k) for k in (1, -1, 2, -2)]
    for device in greeted:
        pl.semaphore_signal(barrier, inc=1, device_id=device, device_id_type=MESH)

    per_device = force_ref.shape[0]
    row_lane = lax.broadcasted_iota(jnp.int32, (1, LANES), 1) - per_device * field
    row = jnp.zeros((1, LANES), jnp.float32)
    for i in range(per_device):
        row = jnp.where(row_lane == i, force_ref[i], row)
    frow_ref[...] = row
    owners = [adv_ref[i] for i in range(PPD)]

    def find_patch(d, carry):
        found = jnp.int32(PPD)
        for i in range(PPD):
            found = jnp.where(owners[i] == d, jnp.int32(i), found)
        inv_ref[d] = found
        return carry

    lax.fori_loop(0, nz * ny, find_patch, 0)
    cells.wait()

    def build_hot(row, carry):
        zrow = lax.div(row, ny)
        yrow = lax.rem(row, ny)
        cell = pc_ref[pl.ds(row, 1), :]
        q = cell // (x_side * AREA)
        inside = cell % (x_side * AREA)
        plane = lax.div(q, PPD) * x_side + lax.div(inside, AREA)
        lp = lax.rem(q, PPD)
        cell_in_plane = lax.rem(inside, AREA)
        e = plane - (line * PLANES - 6)
        m = (lax.div(cell_in_plane, 256) * REGION + e) * PPD + lp
        m = jnp.where((e >= 0) & (e < REGION), m, -1)
        n = lax.rem(cell_in_plane, 256)
        lanes = pl.ds(pl.multiple_of(yrow * LANES, LANES), LANES)
        rows = lax.broadcasted_iota(jnp.int32, (ROWS_HOT, LANES), 0)
        hot_a[zrow, :, lanes] = jnp.where(rows == m, 1.0, 0.0).astype(jnp.bfloat16)
        columns = lax.broadcasted_iota(jnp.int32, (256, LANES), 0)
        hot_b[zrow, :, lanes] = jnp.where(columns == n, 1.0, 0.0).astype(jnp.bfloat16)
        return carry

    half = nz * ny // 2
    lax.fori_loop(0, half, build_hot, 0)
    for copy in loads:
        copy.wait()
    pl.semaphore_wait(barrier, len(greeted))

    def send(source, target, s_sem, r_sem, device):
        copy = pltpu.make_async_remote_copy(
            src_ref=source,
            dst_ref=target,
            send_sem=s_sem,
            recv_sem=r_sem,
            device_id=device,
            device_id_type=MESH,
        )
        copy.start()
        return copy

    x_copies = [
        send(frow_ref, xbuf.at[field], x_send.at[k - 1], x_recv.at[k - 1], along_x(k))
        for k in range(1, nf)
    ]
    halo = []
    for i, (k, lo, hi, dlo, dhi) in enumerate(
        ((1, 0, 4, 0, 4), (-1, 0, 4, 0, 4), (2, 1, 4, 2, 4), (-2, 0, 3, 0, 2))
    ):
        there = along_line(k)
        slot = 2 - k
        halo.append(
            send(
                pa.at[2, lo + 1 : hi + 1],
                pa.at[slot, lo + 1 : hi + 1],
                halo_send.at[0, i],
                halo_recv.at[0, i],
                there,
            )
        )
        halo.append(
            send(
                src.at[2, dlo:dhi],
                src.at[slot, dlo:dhi],
                halo_send.at[1, i],
                halo_recv.at[1, i],
                there,
            )
        )
        halo.append(
            send(tabs.at[2], tabs.at[slot], halo_send.at[2, i], halo_recv.at[2, i], there)
        )

    lax.fori_loop(half, nz * ny, build_hot, 0)

    for copy in x_copies:
        copy.wait_recv()
    row = frow_ref[...]
    for k in range(1, nf):
        row = row + xbuf[lax.rem(field + k, nf)]
    ybuf[y_me] = row
    y_copies = [
        send(ybuf.at[y_me], ybuf.at[y_me], y_send.at[k - 1], y_recv.at[k - 1], along_y(k))
        for k in range(1, ny)
    ]
    acc[...] = jnp.zeros_like(acc)
    for copy in y_copies:
        copy.wait_recv()
    z_copies = [
        send(ybuf, forces.at[z_me], z_send.at[k - 1], z_recv.at[k - 1], along_z(k))
        for k in range(1, nz)
    ]
    forces[z_me] = ybuf[...]

    def add_points(zrow):
        for part in range(2):
            for yrow in range(ny):
                force = forces[zrow, yrow]
                high = force.astype(jnp.bfloat16)
                if part == 1:
                    high = (force - high.astype(jnp.float32)).astype(jnp.bfloat16)
                wide = jnp.broadcast_to(high.astype(jnp.float32), (16, LANES)).astype(jnp.bfloat16)
                for b in range(16):
                    scaled[b * 16 : (b + 1) * 16, yrow * LANES : (yrow + 1) * LANES] = (
                        hot_b[zrow, b * 16 : (b + 1) * 16, yrow * LANES : (yrow + 1) * LANES] * wide
                    )
            acc[...] += lax.dot_general(
                hot_a[zrow],
                scaled[...],
                (((1,), (1,)), ((), ())),
                preferred_element_type=jnp.float32,
            )

    add_points(z_me)

    for copy in halo:
        copy.wait_recv()
    zero_idx = jnp.zeros((PPD, LANES), jnp.int32)
    own_row = lax.broadcasted_iota(jnp.int32, (PPD, LANES), 0)
    z_lane = lane_iota() % SIDE
    for k in range(SLABS):
        table = tabs[k]
        columns = [zero_idx + table[:, c : c + 1] for c in range(6)]
        fk = lax.rem(field + (k - 2 + nf), nf)
        idx[k, 0] = jnp.where(fk == 0, columns[0], own_row)
        idx[k, 1] = jnp.where(fk == nf - 1, columns[1], own_row)
        idx[k, 2] = columns[2] & (PPD - 1)
        idx[k, 3] = columns[3] & (PPD - 1)
        idx[k, 4] = jnp.where(z_lane == 0, columns[4], columns[5]) & (PPD - 1)

    def fill_ghosts(ref, edges):
        for k in edges:
            west, east = idx[k, 0], idx[k - 1, 1]
            west_values = chunks_of(ref, k - 1, PLANES)
            east_values = chunks_of(ref, k, 1)
            for v in range(CHUNKS):
                lanes = slice(v * LANES, (v + 1) * LANES)
                ref[k, 0, :, lanes] = jnp.where(
                    west >= 0, by_patch(west_values[v], west & (PPD - 1)), 0.0
                )
                ref[k - 1, PLANES + 1, :, lanes] = jnp.where(
                    east >= 0, by_patch(east_values[v], east & (PPD - 1)), 0.0
                )

    def sweep(old, new, lo, hi):
        def body(g, carry):
            k = lax.div(g, PLANES)
            j = lax.rem(g, PLANES)
            west = chunks_of(old, k, j)
            center = chunks_of(old, k, j + 1)
            east = chunks_of(old, k, j + 2)
            south, north, below, above, _ = side_values(center, idx[k, 2], idx[k, 3], idx[k, 4])
            for v in range(CHUNKS):
                around = west[v] + east[v] + south[v] + north[v] + below[v] + above[v]
                source = src[k, j, :, v * LANES : (v + 1) * LANES]
                new[k, j + 1, :, v * LANES : (v + 1) * LANES] = center[v] + relaxation * (
                    source - (6.0 * center[v] - around)
                )
            return carry

        lax.fori_loop(lo, hi + 1, body, 0)

    fill_ghosts(pa, range(1, SLABS))
    for copy in halo:
        copy.wait_send()
    sweep(pa, pb, 2, 17)

    for k in range(1, nz):
        z_copies[k - 1].wait_recv()
        add_points(lax.rem(z_me + (nz - k), nz))

    for e in range(REGION):
        k, j = divmod(e + 2, PLANES)
        for part in range(AREA // 256):
            extra = acc[(part * REGION + e) * PPD : (part * REGION + e + 1) * PPD, :]
            lanes = slice(part * 256, (part + 1) * 256)
            src[k, j, :, lanes] += extra
            pb[k, j + 1, :, lanes] += relaxation * extra

    refs = (pa, pb)
    for t in range(2, SWEEPS + 1):
        old, new = refs[(t + 1) % 2], refs[t % 2]
        reach = SWEEPS - t
        fill_ghosts(old, range(1, SLABS) if reach >= 1 else (2, 3))
        sweep(old, new, 7 - reach, 12 + reach)
    final = refs[SWEEPS % 2]
    fill_ghosts(final, (2, 3))

    values = [chunks_of(final, 2, r) for r in range(PLANES + 2)]
    level = values[1][0]
    for r in range(1, PLANES + 1):
        for v in range(CHUNKS):
            if (r, v) != (1, 0):
                level = level + values[r][v]
    level = jnp.sum(level, axis=1, keepdims=True) * (1.0 / (PLANES * AREA))
    lane = lane_iota()
    group = lane // SIDE
    within = lane % SIDE
    chunk_of_lane = within // 4
    face_lane = (within % 4) * SIDE + jnp.where(group == 2, SIDE - 1, 0)
    for r in range(PLANES + 2):
        for v in range(CHUNKS):
            packed[:PPD, r, v, :] = values[r][v] - level
    for r in range(1, PLANES + 1):
        south, north, _, _, faces = side_values(values[r], idx[2, 2], idx[2, 3], idx[2, 4])
        row = jnp.where(group == 0, south[0], north[CHUNKS - 1])
        for v in range(CHUNKS):
            use = (chunk_of_lane == v) & ((group == 1) | (group == 2))
            row = jnp.where(use, by_lane(faces[v], face_lane), row)
        packed[:PPD, PLANES + 2, r - 1, :] = row - level
        packed[:PPD, PLANES + 2, PLANES + r - 1, :] = jnp.zeros_like(row)
    packed[PPD] = jnp.zeros_like(packed[PPD])

    def fill_slot(d, carry):
        sbuf[d] = packed[inv_ref[d]].astype(jnp.bfloat16)
        return carry

    lax.fori_loop(0, nz * ny, fill_slot, 0)

    def shift_of(i):
        a, b = lax.div(i, ny), lax.rem(i, ny)
        return lax.rem(a + b, nz), b

    def remap_copy(i):
        dz, dy = shift_of(i)
        there = lax.rem(z_me + dz, nz) * ny + lax.rem(y_me + dy, ny)
        return pltpu.make_async_remote_copy(
            src_ref=sbuf.at[there],
            dst_ref=rbuf.at[patch],
            send_sem=a_send.at[i],
            recv_sem=a_recv.at[i],
            device_id=(there, field),
            device_id_type=MESH,
        )

    def start_copy(i, carry):
        remap_copy(i).start()
        return carry

    lax.fori_loop(1, nz * ny, start_copy, 0)

    chunk = lax.broadcasted_iota(jnp.int32, (CHUNKS, LANES), 0)
    z = lane % SIDE
    spread_lane = jnp.where(z == 0, SIDE, 2 * SIDE) + chunk * 4 + lane // SIDE
    low_corner = (chunk == 0) & (lane < SIDE)
    high_corner = (chunk == CHUNKS - 1) & (lane >= LANES - SIDE)

    def write_out(s):
        return pltpu.make_async_copy(stage.at[s], out_ref.at[s], out_sem.at[s])

    def form_gradient(ref, s):
        rows = [ref[s, r].astype(jnp.float32) for r in range(PLANES + 3)]
        for x in range(PLANES):
            center = rows[x + 1]
            face = jnp.broadcast_to(rows[PLANES + 2][x : x + 1, :], (CHUNKS, LANES))
            face_z = by_lane(face, spread_lane)
            up = pltpu.roll(center, SIDE, 1)
            down = pltpu.roll(center, LANES - SIDE, 1)
            south = jnp.where(lane < SIDE, pltpu.roll(up, 1, 0), up)
            south = jnp.where(low_corner, face, south)
            north = jnp.where(lane >= LANES - SIDE, pltpu.roll(down, CHUNKS - 1, 0), down)
            north = jnp.where(high_corner, face, north)
            below = jnp.where(z == 0, face_z, pltpu.roll(center, 1, 1))
            above = jnp.where(z == SIDE - 1, face_z, pltpu.roll(center, LANES - 1, 1))
            turn[0, x] = 0.5 * (rows[x + 2] - rows[x])
            turn[1, x] = 0.5 * (north - south)
            turn[2, x] = 0.5 * (above - below)
        for c in range(3):
            for v in range(CHUNKS):
                stage[s, c, :, v * LANES : (v + 1) * LANES] = turn[c, :, v, :].astype(jnp.bfloat16)
        write_out(s).start()

    rbuf[patch] = sbuf[patch]
    form_gradient(rbuf, patch)

    def take_slot(i, carry):
        remap_copy(i).wait_recv()
        dz, dy = shift_of(i)
        origin = lax.rem(z_me + nz - dz, nz) * ny + lax.rem(y_me + ny - dy, ny)
        form_gradient(rbuf, origin)
        return carry

    lax.fori_loop(1, nz * ny, take_slot, 0)

    def end_copy(i, carry):
        remap_copy(i).wait_send()
        return carry

    def end_write(s, carry):
        write_out(s).wait()
        return carry

    for copy in x_copies + y_copies + z_copies:
        copy.wait_send()
    lax.fori_loop(1, nz * ny, end_copy, 0)
    lax.fori_loop(0, nz * ny, end_write, 0)


def on_device(pressure_start, divergence, neighbors, advect_slot, point_cell, point_force):
    n_patch = lax.axis_size("patch")
    nf = lax.axis_size("field")
    ny = math.isqrt(n_patch)
    nz = n_patch // ny
    cells = point_cell.reshape(n_patch, -1)
    if cells.shape[1] < LANES:
        cells = jnp.pad(cells, ((0, 0), (0, LANES - cells.shape[1])), constant_values=-1)

    far = pl.BlockSpec(memory_space=pltpu.HBM)
    smem = pl.BlockSpec(memory_space=pltpu.SMEM)
    dma = pltpu.SemaphoreType.DMA
    slot = (PLANES + 3, CHUNKS, LANES)
    return pl.pallas_call(
        functools.partial(step_kernel, nz, ny, nf),
        out_shape=jax.ShapeDtypeStruct((n_patch, 3, PLANES, AREA), jnp.bfloat16),
        in_specs=[smem, smem, far, far, far, far],
        out_specs=far,
        scratch_shapes=[
            pltpu.SMEM((n_patch,), jnp.int32),
            pltpu.VMEM((1, LANES), jnp.float32),
            pltpu.VMEM((n_patch, LANES), jnp.int32),
            pltpu.VMEM((n_patch,) + slot, jnp.bfloat16),
            pltpu.VMEM((3, PLANES, CHUNKS, LANES), jnp.float32),
            pltpu.VMEM((n_patch, 3, PLANES, AREA), jnp.bfloat16),
            pltpu.VMEM((SLABS, PLANES + 2, PPD, AREA), jnp.float32),
            pltpu.VMEM((SLABS, PLANES + 2, PPD, AREA), jnp.float32),
            pltpu.VMEM((SLABS, PLANES, PPD, AREA), jnp.float32),
            pltpu.VMEM((SLABS, PPD, 6), jnp.int32),
            pltpu.VMEM((nf, 1, LANES), jnp.float32),
            pltpu.VMEM((ny, 1, LANES), jnp.float32),
            pltpu.VMEM((nz, ny, 1, LANES), jnp.float32),
            pltpu.VMEM((nz, ROWS_HOT, ny * LANES), jnp.bfloat16),
            pltpu.VMEM((nz, 256, ny * LANES), jnp.bfloat16),
            pltpu.VMEM((256, ny * LANES), jnp.bfloat16),
            pltpu.VMEM((ROWS_HOT, 256), jnp.float32),
            pltpu.VMEM((SLABS, 5, PPD, LANES), jnp.int32),
            pltpu.VMEM((PPD + 1,) + slot, jnp.float32),
            pltpu.VMEM((n_patch,) + slot, jnp.bfloat16),
            dma((2, PLANES + 1)),
            dma((3, 4)),
            dma((3, 4)),
            dma((nf - 1,)),
            dma((nf - 1,)),
            dma((ny - 1,)),
            dma((ny - 1,)),
            dma((nz - 1,)),
            dma((nz - 1,)),
            dma((n_patch,)),
            dma((n_patch,)),
            dma((n_patch,)),
        ],
        compiler_params=pltpu.CompilerParams(
            collective_id=0, has_side_effects=True, vmem_limit_bytes=67043328
        ),
        name="step",
    )(advect_slot, point_force, pressure_start, divergence, neighbors, cells)


def solution(mesh):
    in_specs = (
        P("patch", "field", None),
        P("patch", "field", None),
        P("patch", None),
        P("patch"),
        P(),
        P(("patch", "field")),
    )
    out_specs = P("patch", None, "field", None)
    return jax.shard_map(
        on_device, mesh=mesh, in_specs=in_specs, out_specs=out_specs, check_vma=False
    )
```

```python
import functools
import math

import jax
import jax.numpy as jnp
from jax import lax
from jax.experimental import pallas as pl
from jax.experimental.pallas import tpu as pltpu
from jax.sharding import PartitionSpec as P

SIDE = 32
SWEEPS = 6
PPD = 8
PLANES = 4
AREA = SIDE * SIDE
CHUNKS = AREA // 128
SLABS = 5
LANES = 128
REGION = 16
ROWS_HOT = REGION * PPD * (AREA // 256)
MESH = pl.DeviceIdType.MESH

relaxation = 1.0 / 9.0


def lane_iota():
    return lax.broadcasted_iota(jnp.int32, (PPD, LANES), 1)


def by_patch(value, index):
    return jnp.take_along_axis(value, index, axis=0, mode="promise_in_bounds")


def by_lane(value, index):
    return jnp.take_along_axis(value, index, axis=1, mode="promise_in_bounds")


def side_values(center, idx_south, idx_north, idx_z):
    lane = lane_iota()
    z = lane % SIDE
    up = [pltpu.roll(c, SIDE, 1) for c in center]
    down = [pltpu.roll(c, LANES - SIDE, 1) for c in center]
    first = by_patch(up[CHUNKS - 1], idx_south)
    last = by_patch(down[0], idx_north)
    south, north, below, above, faces = [], [], [], [], []
    for v in range(CHUNKS):
        south.append(jnp.where(lane < SIDE, first if v == 0 else up[v - 1], up[v]))
        north.append(
            jnp.where(lane >= LANES - SIDE, last if v == CHUNKS - 1 else down[v + 1], down[v])
        )
        swapped = jnp.where(
            z == 0,
            pltpu.roll(center[v], LANES - (SIDE - 1), 1),
            pltpu.roll(center[v], SIDE - 1, 1),
        )
        face = by_patch(swapped, idx_z)
        faces.append(face)
        below.append(jnp.where(z == 0, face, pltpu.roll(center[v], 1, 1)))
        above.append(jnp.where(z == SIDE - 1, face, pltpu.roll(center[v], LANES - 1, 1)))
    return south, north, below, above, faces


def chunks_of(ref, k, row):
    return [ref[k, row, :, v * LANES : (v + 1) * LANES] for v in range(CHUNKS)]


def step_kernel(
    nz,
    ny,
    nf,
    adv_ref,
    force_ref,
    p_ref,
    d_ref,
    tab_ref,
    cell_ref,
    out_ref,
    inv_ref,
    frow_ref,
    pc_ref,
    rbuf,
    turn,
    adv_smem,
    force_smem,
    pa,
    pb,
    src,
    tabs,
    xbuf,
    ybuf,
    forces,
    hot_a,
    hot_b,
    scaled,
    acc,
    idx,
    packed,
    sbuf,
    load_sem,
    halo_send,
    halo_recv,
    x_send,
    x_recv,
    y_send,
    y_recv,
    z_send,
    z_recv,
    a_send,
    a_recv,
    out_sem,
):
    patch = lax.axis_index("patch")
    field = lax.axis_index("field")
    z_me = lax.div(patch, ny)
    y_me = lax.rem(patch, ny)
    total = nz * ny * nf
    line = patch * nf + field
    x_side = PLANES * nf

    def along_line(k):
        other = lax.rem(line + (k + total), total)
        return (lax.div(other, nf), lax.rem(other, nf))

    def along_x(k):
        return (patch, lax.rem(field + k, nf))

    def along_y(k):
        return (z_me * ny + lax.rem(y_me + k, ny), field)

    def along_z(k):
        return (lax.rem(z_me + k, nz) * ny + y_me, field)

    loads = []
    for x in range(PLANES):
        loads.append(
            pltpu.make_async_copy(p_ref.at[:, x, :], pa.at[2, x + 1], load_sem.at[0, x])
        )
        loads.append(pltpu.make_async_copy(d_ref.at[:, x, :], src.at[2, x], load_sem.at[1, x]))
    loads.append(pltpu.make_async_copy(tab_ref, tabs.at[2], load_sem.at[0, PLANES]))
    small = [
        pltpu.make_async_copy(force_ref, force_smem, out_sem.at[0]),
        pltpu.make_async_copy(adv_ref, adv_smem, out_sem.at[1]),
    ]
    for copy in small:
        copy.start()
    cells = pltpu.make_async_copy(cell_ref, pc_ref, load_sem.at[1, PLANES])
    cells.start()
    for copy in loads:
        copy.start()

    barrier = pltpu.get_barrier_semaphore()
    greeted = [along_x(k) for k in range(1, nf)]
    greeted += [along_y(k) for k in range(1, ny)]
    greeted += [along_z(k) for k in range(1, nz)]
    greeted += [along_line(k) for k in (1, -1, 2, -2)]
    for device in greeted:
        pl.semaphore_signal(barrier, inc=1, device_id=device, device_id_type=MESH)

    per_device = force_ref.shape[0]
    row_lane = lax.broadcasted_iota(jnp.int32, (1, LANES), 1) - per_device * field
    row = jnp.zeros((1, LANES), jnp.float32)
    for copy in small:
        copy.wait()
    for i in range(per_device):
        row = jnp.where(row_lane == i, force_smem[i], row)
    frow_ref[...] = row
    owners = [adv_smem[i] for i in range(PPD)]

    def find_patch(d, carry):
        found = jnp.int32(PPD)
        for i in range(PPD):
            found = jnp.where(owners[i] == d, jnp.int32(i), found)
        inv_ref[d] = found
        return carry


    base_rows = lax.broadcasted_iota(jnp.int32, (16, LANES), 0).astype(jnp.float32).astype(jnp.bfloat16)

    def build_hot(row, carry):
        zrow = lax.div(row, ny)
        yrow = lax.rem(row, ny)
        cell = pc_ref[pl.ds(row, 1), :]
        q = cell // (x_side * AREA)
        inside = cell % (x_side * AREA)
        plane = lax.div(q, PPD) * x_side + lax.div(inside, AREA)
        lp = lax.rem(q, PPD)
        cell_in_plane = lax.rem(inside, AREA)
        e = plane - (line * PLANES - 6)
        m = (lax.div(cell_in_plane, 256) * REGION + e) * PPD + lp
        m = jnp.where((e >= 0) & (e < REGION), m, -1)
        n = lax.rem(cell_in_plane, 256)
        lanes = pl.ds(pl.multiple_of(yrow * LANES, LANES), LANES)
        def one_hot(place, size):
            at = jnp.clip(place, -1, 256).astype(jnp.float32)
            at = jnp.broadcast_to(at, (16, LANES)).astype(jnp.bfloat16)
            one = jnp.ones((16, LANES), jnp.bfloat16)
            return [
                jnp.where(base_rows + jnp.bfloat16(16 * b) == at, one, one - one)
                for b in range(size // 16)
            ]

        for part in range(ROWS_HOT // 256):
            for b, block in enumerate(one_hot(m - 256 * part, 256)):
                hot_a[zrow, part * 256 + b * 16 : part * 256 + (b + 1) * 16, lanes] = block
        for b, block in enumerate(one_hot(n, 256)):
            hot_b[zrow, b * 16 : (b + 1) * 16, lanes] = block
        return carry

    pl.semaphore_wait(barrier, len(greeted))

    def send(source, target, s_sem, r_sem, device):
        copy = pltpu.make_async_remote_copy(
            src_ref=source,
            dst_ref=target,
            send_sem=s_sem,
            recv_sem=r_sem,
            device_id=device,
            device_id_type=MESH,
        )
        copy.start()
        return copy

    x_copies = [
        send(frow_ref, xbuf.at[field], x_send.at[k - 1], x_recv.at[k - 1], along_x(k))
        for k in range(1, nf)
    ]
    for copy in loads:
        copy.wait()
    halo = []
    for i, (k, lo, hi, dlo, dhi) in enumerate(
        ((1, 0, 4, 0, 4), (-1, 0, 4, 0, 4), (2, 1, 4, 2, 4), (-2, 0, 3, 0, 2))
    ):
        there = along_line(k)
        slot = 2 - k
        halo.append(
            send(
                pa.at[2, lo + 1 : hi + 1],
                pa.at[slot, lo + 1 : hi + 1],
                halo_send.at[0, i],
                halo_recv.at[0, i],
                there,
            )
        )
        halo.append(
            send(
                src.at[2, dlo:dhi],
                src.at[slot, dlo:dhi],
                halo_send.at[1, i],
                halo_recv.at[1, i],
                there,
            )
        )
        halo.append(
            send(tabs.at[2], tabs.at[slot], halo_send.at[2, i], halo_recv.at[2, i], there)
        )

    half = nz * ny // 2
    cells.wait()
    lax.fori_loop(0, half, build_hot, 0)

    for copy in x_copies:
        copy.wait_recv()
    row = frow_ref[...]
    for k in range(1, nf):
        row = row + xbuf[lax.rem(field + k, nf)]
    ybuf[y_me] = row
    y_copies = [
        send(ybuf.at[y_me], ybuf.at[y_me], y_send.at[k - 1], y_recv.at[k - 1], along_y(k))
        for k in range(1, ny)
    ]
    acc[...] = jnp.zeros_like(acc)
    lax.fori_loop(half, nz * ny, build_hot, 0)
    lax.fori_loop(0, nz * ny, find_patch, 0)
    for copy in y_copies:
        copy.wait_recv()
    z_copies = [
        send(ybuf, forces.at[z_me], z_send.at[k - 1], z_recv.at[k - 1], along_z(k))
        for k in range(1, nz)
    ]
    forces[z_me] = ybuf[...]

    def add_points(zrow):
        for yrow in range(ny):
            lanes = slice(yrow * LANES, (yrow + 1) * LANES)
            wide = jnp.broadcast_to(forces[zrow, yrow], (16, LANES)).astype(jnp.bfloat16)
            for b in range(16):
                rows = slice(b * 16, (b + 1) * 16)
                scaled[rows, lanes] = hot_b[zrow, rows, lanes] * wide
        acc[...] += lax.dot_general(
            hot_a[zrow],
            scaled[...],
            (((1,), (1,)), ((), ())),
            preferred_element_type=jnp.float32,
        )

    add_points(z_me)

    for copy in halo:
        copy.wait_recv()
    zero_idx = jnp.zeros((PPD, LANES), jnp.int32)
    own_row = lax.broadcasted_iota(jnp.int32, (PPD, LANES), 0)
    z_lane = lane_iota() % SIDE
    for k in range(SLABS):
        table = tabs[k]
        columns = [zero_idx + table[:, c : c + 1] for c in range(6)]
        fk = lax.rem(field + (k - 2 + nf), nf)
        idx[k, 0] = jnp.where(fk == 0, columns[0], own_row)
        idx[k, 1] = jnp.where(fk == nf - 1, columns[1], own_row)
        idx[k, 2] = columns[2] & (PPD - 1)
        idx[k, 3] = columns[3] & (PPD - 1)
        idx[k, 4] = jnp.where(z_lane == 0, columns[4], columns[5]) & (PPD - 1)

    def fill_ghosts(ref, edges):
        for k in edges:
            west, east = idx[k, 0], idx[k - 1, 1]
            west_values = chunks_of(ref, k - 1, PLANES)
            east_values = chunks_of(ref, k, 1)
            for v in range(CHUNKS):
                lanes = slice(v * LANES, (v + 1) * LANES)
                ref[k, 0, :, lanes] = jnp.where(
                    west >= 0, by_patch(west_values[v], west & (PPD - 1)), 0.0
                )
                ref[k - 1, PLANES + 1, :, lanes] = jnp.where(
                    east >= 0, by_patch(east_values[v], east & (PPD - 1)), 0.0
                )

    def sweep(old, new, lo, hi):
        def relax(g):
            k = lax.div(g, PLANES)
            j = lax.rem(g, PLANES)
            west = chunks_of(old, k, j)
            center = chunks_of(old, k, j + 1)
            east = chunks_of(old, k, j + 2)
            south, north, below, above, _ = side_values(center, idx[k, 2], idx[k, 3], idx[k, 4])
            result = []
            for v in range(CHUNKS):
                around = west[v] + east[v] + south[v] + north[v] + below[v] + above[v]
                source = src[k, j, :, v * LANES : (v + 1) * LANES]
                result.append(center[v] + relaxation * (source - (6.0 * center[v] - around)))
            return k, j, result

        def body(i, carry):
            done = [relax(lo + 2 * i), relax(lo + 2 * i + 1)]
            for k, j, result in done:
                for v in range(CHUNKS):
                    new[k, j + 1, :, v * LANES : (v + 1) * LANES] = result[v]
            return carry

        lax.fori_loop(0, (hi + 1 - lo) // 2, body, 0)

    fill_ghosts(pa, range(1, SLABS))
    for copy in halo:
        copy.wait_send()
    sweep(pa, pb, 2, 17)

    for k in range(1, nz):
        z_copies[k - 1].wait_recv()
        add_points(lax.rem(z_me + (nz - k), nz))

    for e in range(REGION):
        k, j = divmod(e + 2, PLANES)
        for part in range(AREA // 256):
            extra = acc[(part * REGION + e) * PPD : (part * REGION + e + 1) * PPD, :]
            lanes = slice(part * 256, (part + 1) * 256)
            src[k, j, :, lanes] += extra
            pb[k, j + 1, :, lanes] += relaxation * extra

    refs = (pa, pb)
    for t in range(2, SWEEPS + 1):
        old, new = refs[(t + 1) % 2], refs[t % 2]
        reach = SWEEPS - t
        fill_ghosts(old, range(1, SLABS) if reach >= 1 else (2, 3))
        sweep(old, new, 7 - reach, 12 + reach)
    final = refs[SWEEPS % 2]
    fill_ghosts(final, (2, 3))

    values = [chunks_of(final, 2, r) for r in range(PLANES + 2)]
    level = values[1][0]
    for r in range(1, PLANES + 1):
        for v in range(CHUNKS):
            if (r, v) != (1, 0):
                level = level + values[r][v]
    level = jnp.sum(level, axis=1, keepdims=True) * (1.0 / (PLANES * AREA))
    lane = lane_iota()
    group = lane // SIDE
    within = lane % SIDE
    chunk_of_lane = within // 4
    face_lane = (within % 4) * SIDE + jnp.where(group == 2, SIDE - 1, 0)
    for r in range(PLANES + 2):
        for v in range(CHUNKS):
            packed[:PPD, r, v, :] = values[r][v] - level
    for r in range(1, PLANES + 1):
        south, north, _, _, faces = side_values(values[r], idx[2, 2], idx[2, 3], idx[2, 4])
        row = jnp.where(group == 0, south[0], north[CHUNKS - 1])
        for v in range(CHUNKS):
            use = (chunk_of_lane == v) & ((group == 1) | (group == 2))
            row = jnp.where(use, by_lane(faces[v], face_lane), row)
        packed[:PPD, PLANES + 2, r - 1, :] = row - level
        packed[:PPD, PLANES + 2, PLANES + r - 1, :] = jnp.zeros_like(row)
    packed[PPD] = jnp.zeros_like(packed[PPD])

    def fill_slot(d, carry):
        sbuf[d] = packed[inv_ref[d]].astype(jnp.bfloat16)
        return carry

    lax.fori_loop(0, nz * ny, fill_slot, 0)

    def shift_of(i):
        a, b = lax.div(i, ny), lax.rem(i, ny)
        return lax.rem(a + b, nz), b

    def remap_copy(i):
        dz, dy = shift_of(i)
        there = lax.rem(z_me + dz, nz) * ny + lax.rem(y_me + dy, ny)
        return pltpu.make_async_remote_copy(
            src_ref=sbuf.at[there],
            dst_ref=rbuf.at[patch],
            send_sem=a_send.at[i],
            recv_sem=a_recv.at[i],
            device_id=(there, field),
            device_id_type=MESH,
        )

    def start_copy(i, carry):
        remap_copy(i).start()
        return carry

    lax.fori_loop(1, nz * ny, start_copy, 0)

    chunk = lax.broadcasted_iota(jnp.int32, (CHUNKS, LANES), 0)
    z = lane % SIDE
    spread_lane = jnp.where(z == 0, SIDE, 2 * SIDE) + chunk * 4 + lane // SIDE
    low_corner = (chunk == 0) & (lane < SIDE)
    high_corner = (chunk == CHUNKS - 1) & (lane >= LANES - SIDE)

    def form_gradient(ref, s):
        rows = [ref[s, r].astype(jnp.float32) for r in range(PLANES + 3)]
        for x in range(PLANES):
            center = rows[x + 1]
            face = jnp.broadcast_to(rows[PLANES + 2][x : x + 1, :], (CHUNKS, LANES))
            face_z = by_lane(face, spread_lane)
            up = pltpu.roll(center, SIDE, 1)
            down = pltpu.roll(center, LANES - SIDE, 1)
            south = jnp.where(lane < SIDE, pltpu.roll(up, 1, 0), up)
            south = jnp.where(low_corner, face, south)
            north = jnp.where(lane >= LANES - SIDE, pltpu.roll(down, CHUNKS - 1, 0), down)
            north = jnp.where(high_corner, face, north)
            below = jnp.where(z == 0, face_z, pltpu.roll(center, 1, 1))
            above = jnp.where(z == SIDE - 1, face_z, pltpu.roll(center, LANES - 1, 1))
            turn[0, x] = 0.5 * (rows[x + 2] - rows[x])
            turn[1, x] = 0.5 * (north - south)
            turn[2, x] = 0.5 * (above - below)
        for c in range(3):
            for v in range(CHUNKS):
                out_ref[s, c, :, v * LANES : (v + 1) * LANES] = turn[c, :, v, :].astype(jnp.bfloat16)

    rbuf[patch] = sbuf[patch]
    form_gradient(rbuf, patch)

    def take_slot(i, carry):
        remap_copy(i).wait_recv()
        dz, dy = shift_of(i)
        origin = lax.rem(z_me + nz - dz, nz) * ny + lax.rem(y_me + ny - dy, ny)
        form_gradient(rbuf, origin)
        return carry

    lax.fori_loop(1, nz * ny, take_slot, 0)

    def end_copy(i, carry):
        remap_copy(i).wait_send()
        return carry

    for copy in x_copies + y_copies + z_copies:
        copy.wait_send()
    lax.fori_loop(1, nz * ny, end_copy, 0)


def on_device(pressure_start, divergence, neighbors, advect_slot, point_cell, point_force):
    n_patch = lax.axis_size("patch")
    nf = lax.axis_size("field")
    ny = math.isqrt(n_patch)
    nz = n_patch // ny
    cells = point_cell.reshape(n_patch, -1)
    if cells.shape[1] < LANES:
        cells = jnp.pad(cells, ((0, 0), (0, LANES - cells.shape[1])), constant_values=-1)

    far = pl.BlockSpec(memory_space=pltpu.HBM)
    dma = pltpu.SemaphoreType.DMA
    slot = (PLANES + 3, CHUNKS, LANES)
    inputs = (advect_slot, point_force, pressure_start, divergence, neighbors, cells)
    return pl.pallas_call(
        functools.partial(step_kernel, nz, ny, nf),
        out_shape=jax.ShapeDtypeStruct((n_patch, 3, PLANES, AREA), jnp.bfloat16),
        in_specs=[far, far, far, far, far, far],
        out_specs=pl.BlockSpec(memory_space=pltpu.VMEM),
        scratch_shapes=[
            pltpu.SMEM((n_patch,), jnp.int32),
            pltpu.VMEM((1, LANES), jnp.float32),
            pltpu.VMEM((n_patch, LANES), jnp.int32),
            pltpu.VMEM((n_patch,) + slot, jnp.bfloat16),
            pltpu.VMEM((3, PLANES, CHUNKS, LANES), jnp.float32),
            pltpu.SMEM(advect_slot.shape, jnp.int32),
            pltpu.SMEM(point_force.shape, jnp.float32),
            pltpu.VMEM((SLABS, PLANES + 2, PPD, AREA), jnp.float32),
            pltpu.VMEM((SLABS, PLANES + 2, PPD, AREA), jnp.float32),
            pltpu.VMEM((SLABS, PLANES, PPD, AREA), jnp.float32),
            pltpu.VMEM((SLABS, PPD, 6), jnp.int32),
            pltpu.VMEM((nf, 1, LANES), jnp.float32),
            pltpu.VMEM((ny, 1, LANES), jnp.float32),
            pltpu.VMEM((nz, ny, 1, LANES), jnp.float32),
            pltpu.VMEM((nz, ROWS_HOT, ny * LANES), jnp.bfloat16),
            pltpu.VMEM((nz, 256, ny * LANES), jnp.bfloat16),
            pltpu.VMEM((256, ny * LANES), jnp.bfloat16),
            pltpu.VMEM((ROWS_HOT, 256), jnp.float32),
            pltpu.VMEM((SLABS, 5, PPD, LANES), jnp.int32),
            pltpu.VMEM((PPD + 1,) + slot, jnp.float32),
            pltpu.VMEM((n_patch,) + slot, jnp.bfloat16),
            dma((2, PLANES + 1)),
            dma((3, 4)),
            dma((3, 4)),
            dma((nf - 1,)),
            dma((nf - 1,)),
            dma((ny - 1,)),
            dma((ny - 1,)),
            dma((nz - 1,)),
            dma((nz - 1,)),
            dma((n_patch,)),
            dma((n_patch,)),
            dma((2,)),
        ],
        compiler_params=pltpu.CompilerParams(
            collective_id=0, has_side_effects=True, vmem_limit_bytes=48*1024*1024
        ),
        name="step",
    )(*[pltpu.with_memory_space_constraint(v, pltpu.HBM) for v in inputs])
def solution(mesh):
    in_specs = (
        P("patch", "field", None),
        P("patch", "field", None),
        P("patch", None),
        P("patch"),
        P(),
        P(("patch", "field")),
    )
    out_specs = P("patch", None, "field", None)
    return jax.shard_map(
        on_device, mesh=mesh, in_specs=in_specs, out_specs=out_specs, check_vma=False
    )
```

```python
import functools
import math

import jax
import jax.numpy as jnp
from jax import lax
from jax.experimental import pallas as pl
from jax.experimental.pallas import tpu as pltpu
from jax.sharding import PartitionSpec as P

SIDE = 32
SWEEPS = 6
PPD = 8
PLANES = 4
AREA = SIDE * SIDE
CHUNKS = AREA // 128
SLABS = 5
LANES = 128
REGION = 16
ROWS_HOT = REGION * PPD * (AREA // 256)
MESH = pl.DeviceIdType.MESH

relaxation = 1.0 / 9.0


def lane_iota():
    return lax.broadcasted_iota(jnp.int32, (PPD, LANES), 1)


def by_patch(value, index):
    return jnp.take_along_axis(value, index, axis=0, mode="promise_in_bounds")


def by_lane(value, index):
    return jnp.take_along_axis(value, index, axis=1, mode="promise_in_bounds")


def side_values(center, idx_south, idx_north, idx_z):
    lane = lane_iota()
    z = lane % SIDE
    other_end = jnp.where(
        z == 0, lane + (SIDE - 1), jnp.where(z == SIDE - 1, lane - (SIDE - 1), lane)
    )
    up = [pltpu.roll(c, SIDE, 1) for c in center]
    down = [pltpu.roll(c, LANES - SIDE, 1) for c in center]
    first = by_patch(up[CHUNKS - 1], idx_south)
    last = by_patch(down[0], idx_north)
    south, north, below, above, faces = [], [], [], [], []
    for v in range(CHUNKS):
        south.append(jnp.where(lane < SIDE, first if v == 0 else up[v - 1], up[v]))
        north.append(
            jnp.where(lane >= LANES - SIDE, last if v == CHUNKS - 1 else down[v + 1], down[v])
        )
        swapped = by_lane(center[v], other_end)
        face = by_patch(swapped, idx_z)
        faces.append(face)
        below.append(jnp.where(z == 0, face, pltpu.roll(center[v], 1, 1)))
        above.append(jnp.where(z == SIDE - 1, face, pltpu.roll(center[v], LANES - 1, 1)))
    return south, north, below, above, faces


def chunks_of(ref, k, row):
    return [ref[k, row, :, v * LANES : (v + 1) * LANES] for v in range(CHUNKS)]


def step_kernel(
    nz,
    ny,
    nf,
    adv_ref,
    force_ref,
    p_ref,
    d_ref,
    tab_ref,
    cell_ref,
    out_ref,
    inv_ref,
    frow_ref,
    pc_ref,
    rbuf,
    turn,
    adv_smem,
    force_smem,
    pa,
    pb,
    src,
    tabs,
    xbuf,
    ybuf,
    forces,
    hot_a,
    hot_b,
    scaled,
    acc,
    idx,
    packed,
    sbuf,
    load_sem,
    halo_send,
    halo_recv,
    x_send,
    x_recv,
    y_send,
    y_recv,
    z_send,
    z_recv,
    a_send,
    a_recv,
    out_sem,
):
    patch = lax.axis_index("patch")
    field = lax.axis_index("field")
    z_me = lax.div(patch, ny)
    y_me = lax.rem(patch, ny)
    total = nz * ny * nf
    line = patch * nf + field
    x_side = PLANES * nf

    def along_line(k):
        other = lax.rem(line + (k + total), total)
        return (lax.div(other, nf), lax.rem(other, nf))

    def along_x(k):
        return (patch, lax.rem(field + k, nf))

    def along_y(k):
        return (z_me * ny + lax.rem(y_me + k, ny), field)

    def along_z(k):
        return (lax.rem(z_me + k, nz) * ny + y_me, field)

    loads = []
    for x in range(PLANES):
        loads.append(
            pltpu.make_async_copy(p_ref.at[:, x, :], pa.at[2, x + 1], load_sem.at[0, x])
        )
        loads.append(pltpu.make_async_copy(d_ref.at[:, x, :], src.at[2, x], load_sem.at[1, x]))
    loads.append(pltpu.make_async_copy(tab_ref, tabs.at[2], load_sem.at[0, PLANES]))
    small = [
        pltpu.make_async_copy(force_ref, force_smem, out_sem.at[0]),
        pltpu.make_async_copy(adv_ref, adv_smem, out_sem.at[1]),
    ]
    for copy in small:
        copy.start()
    cells = pltpu.make_async_copy(cell_ref, pc_ref, load_sem.at[1, PLANES])
    cells.start()
    for copy in loads:
        copy.start()

    barrier = pltpu.get_barrier_semaphore()
    greeted = [along_x(k) for k in range(1, nf)]
    greeted += [along_y(k) for k in range(1, ny)]
    greeted += [along_z(k) for k in range(1, nz)]
    greeted += [along_line(k) for k in (1, -1, 2, -2)]
    for device in greeted:
        pl.semaphore_signal(barrier, inc=1, device_id=device, device_id_type=MESH)

    per_device = force_ref.shape[0]
    row_lane = lax.broadcasted_iota(jnp.int32, (1, LANES), 1) - per_device * field
    row = jnp.zeros((1, LANES), jnp.float32)
    for copy in small:
        copy.wait()
    for i in range(per_device):
        row = jnp.where(row_lane == i, force_smem[i], row)
    frow_ref[...] = row
    owners = [adv_smem[i] for i in range(PPD)]

    def find_patch(d, carry):
        found = jnp.int32(PPD)
        for i in range(PPD):
            found = jnp.where(owners[i] == d, jnp.int32(i), found)
        inv_ref[d] = found
        return carry


    base_rows = lax.broadcasted_iota(jnp.int32, (16, LANES), 0).astype(jnp.float32).astype(jnp.bfloat16)

    def build_hot(row, carry):
        zrow = lax.div(row, ny)
        yrow = lax.rem(row, ny)
        cell = pc_ref[pl.ds(row, 1), :]
        q = cell // (x_side * AREA)
        inside = cell % (x_side * AREA)
        plane = lax.div(q, PPD) * x_side + lax.div(inside, AREA)
        lp = lax.rem(q, PPD)
        cell_in_plane = lax.rem(inside, AREA)
        e = plane - (line * PLANES - 6)
        m = (lax.div(cell_in_plane, 256) * REGION + e) * PPD + lp
        m = jnp.where((e >= 0) & (e < REGION), m, -1)
        n = lax.rem(cell_in_plane, 256)
        lanes = pl.ds(pl.multiple_of(yrow * LANES, LANES), LANES)
        def one_hot(place, size):
            at = jnp.clip(place, -1, 256).astype(jnp.float32)
            at = jnp.broadcast_to(at, (16, LANES)).astype(jnp.bfloat16)
            one = jnp.ones((16, LANES), jnp.bfloat16)
            return [
                jnp.where(base_rows + jnp.bfloat16(16 * b) == at, one, one - one)
                for b in range(size // 16)
            ]

        for part in range(ROWS_HOT // 256):
            for b, block in enumerate(one_hot(m - 256 * part, 256)):
                hot_a[zrow, part * 256 + b * 16 : part * 256 + (b + 1) * 16, lanes] = block
        for b, block in enumerate(one_hot(n, 256)):
            hot_b[zrow, b * 16 : (b + 1) * 16, lanes] = block
        return carry

    pl.semaphore_wait(barrier, len(greeted))

    def send(source, target, s_sem, r_sem, device):
        copy = pltpu.make_async_remote_copy(
            src_ref=source,
            dst_ref=target,
            send_sem=s_sem,
            recv_sem=r_sem,
            device_id=device,
            device_id_type=MESH,
        )
        copy.start()
        return copy

    x_copies = [
        send(frow_ref, xbuf.at[field], x_send.at[k - 1], x_recv.at[k - 1], along_x(k))
        for k in range(1, nf)
    ]
    for copy in loads:
        copy.wait()
    halo = []
    for i, (k, lo, hi, dlo, dhi) in enumerate(
        ((1, 0, 4, 0, 4), (-1, 0, 4, 0, 4), (2, 1, 4, 2, 4), (-2, 0, 3, 0, 2))
    ):
        there = along_line(k)
        slot = 2 - k
        halo.append(
            send(
                pa.at[2, lo + 1 : hi + 1],
                pa.at[slot, lo + 1 : hi + 1],
                halo_send.at[0, i],
                halo_recv.at[0, i],
                there,
            )
        )
        halo.append(
            send(
                src.at[2, dlo:dhi],
                src.at[slot, dlo:dhi],
                halo_send.at[1, i],
                halo_recv.at[1, i],
                there,
            )
        )
        halo.append(
            send(tabs.at[2], tabs.at[slot], halo_send.at[2, i], halo_recv.at[2, i], there)
        )

    half = nz * ny // 2
    cells.wait()
    lax.fori_loop(0, half, build_hot, 0)

    for copy in x_copies:
        copy.wait_recv()
    row = frow_ref[...]
    for k in range(1, nf):
        row = row + xbuf[lax.rem(field + k, nf)]
    ybuf[y_me] = row
    y_copies = [
        send(ybuf.at[y_me], ybuf.at[y_me], y_send.at[k - 1], y_recv.at[k - 1], along_y(k))
        for k in range(1, ny)
    ]
    acc[...] = jnp.zeros_like(acc)
    lax.fori_loop(half, nz * ny, build_hot, 0)
    lax.fori_loop(0, nz * ny, find_patch, 0)
    for copy in y_copies:
        copy.wait_recv()
    z_copies = [
        send(ybuf, forces.at[z_me], z_send.at[k - 1], z_recv.at[k - 1], along_z(k))
        for k in range(1, nz)
    ]
    forces[z_me] = ybuf[...]

    def add_points(zrow):
        for yrow in range(ny):
            lanes = slice(yrow * LANES, (yrow + 1) * LANES)
            wide = jnp.broadcast_to(forces[zrow, yrow], (16, LANES)).astype(jnp.bfloat16)
            for b in range(16):
                rows = slice(b * 16, (b + 1) * 16)
                scaled[rows, lanes] = hot_b[zrow, rows, lanes] * wide
        acc[...] += lax.dot_general(
            hot_a[zrow],
            scaled[...],
            (((1,), (1,)), ((), ())),
            preferred_element_type=jnp.float32,
        )

    add_points(z_me)

    for copy in halo:
        copy.wait_recv()
    zero_idx = jnp.zeros((PPD, LANES), jnp.int32)
    own_row = lax.broadcasted_iota(jnp.int32, (PPD, LANES), 0)
    z_lane = lane_iota() % SIDE
    for k in range(SLABS):
        table = tabs[k]
        columns = [zero_idx + table[:, c : c + 1] for c in range(6)]
        fk = lax.rem(field + (k - 2 + nf), nf)
        idx[k, 0] = jnp.where(fk == 0, columns[0], own_row)
        idx[k, 1] = jnp.where(fk == nf - 1, columns[1], own_row)
        idx[k, 2] = columns[2] & (PPD - 1)
        idx[k, 3] = columns[3] & (PPD - 1)
        idx[k, 4] = jnp.where(z_lane == 0, columns[4], columns[5]) & (PPD - 1)

    def fill_ghosts(ref, edges):
        for k in edges:
            west, east = idx[k, 0], idx[k - 1, 1]
            west_values = chunks_of(ref, k - 1, PLANES)
            east_values = chunks_of(ref, k, 1)
            for v in range(CHUNKS):
                lanes = slice(v * LANES, (v + 1) * LANES)
                ref[k, 0, :, lanes] = jnp.where(
                    west >= 0, by_patch(west_values[v], west & (PPD - 1)), 0.0
                )
                ref[k - 1, PLANES + 1, :, lanes] = jnp.where(
                    east >= 0, by_patch(east_values[v], east & (PPD - 1)), 0.0
                )

    def sweep(old, new, lo, hi):
        def relax(g):
            k = lax.div(g, PLANES)
            j = lax.rem(g, PLANES)
            west = chunks_of(old, k, j)
            center = chunks_of(old, k, j + 1)
            east = chunks_of(old, k, j + 2)
            south, north, below, above, _ = side_values(center, idx[k, 2], idx[k, 3], idx[k, 4])
            result = []
            for v in range(CHUNKS):
                around = west[v] + east[v] + south[v] + north[v] + below[v] + above[v]
                source = src[k, j, :, v * LANES : (v + 1) * LANES]
                result.append(center[v] + relaxation * (source - (6.0 * center[v] - around)))
            return k, j, result

        def body(i, carry):
            done = [relax(lo + 2 * i), relax(lo + 2 * i + 1)]
            for k, j, result in done:
                for v in range(CHUNKS):
                    new[k, j + 1, :, v * LANES : (v + 1) * LANES] = result[v]
            return carry

        lax.fori_loop(0, (hi + 1 - lo) // 2, body, 0)

    fill_ghosts(pa, range(1, SLABS))
    for copy in halo:
        copy.wait_send()
    sweep(pa, pb, 2, 17)

    for k in sorted(range(1, nz), key=lambda k: min(k, nz - k)):
        z_copies[k - 1].wait_recv()
        add_points(lax.rem(z_me + (nz - k), nz))

    for e in range(REGION):
        k, j = divmod(e + 2, PLANES)
        for part in range(AREA // 256):
            extra = acc[(part * REGION + e) * PPD : (part * REGION + e + 1) * PPD, :]
            lanes = slice(part * 256, (part + 1) * 256)
            src[k, j, :, lanes] += extra
            pb[k, j + 1, :, lanes] += relaxation * extra

    refs = (pa, pb)
    for t in range(2, SWEEPS + 1):
        old, new = refs[(t + 1) % 2], refs[t % 2]
        reach = SWEEPS - t
        fill_ghosts(old, range(1, SLABS) if reach >= 1 else (2, 3))
        sweep(old, new, 7 - reach, 12 + reach)
    final = refs[SWEEPS % 2]
    fill_ghosts(final, (2, 3))

    values = [chunks_of(final, 2, r) for r in range(PLANES + 2)]
    level = values[1][0]
    for r in range(1, PLANES + 1):
        for v in range(CHUNKS):
            if (r, v) != (1, 0):
                level = level + values[r][v]
    level = jnp.sum(level, axis=1, keepdims=True) * (1.0 / (PLANES * AREA))
    lane = lane_iota()
    group = lane // SIDE
    within = lane % SIDE
    chunk_of_lane = within // 4
    face_lane = (within % 4) * SIDE + jnp.where(group == 2, SIDE - 1, 0)
    for r in range(PLANES + 2):
        for v in range(CHUNKS):
            packed[:PPD, 2 * r + v // 4, v % 4, :] = values[r][v] - level
    for r in range(1, PLANES + 1):
        south, north, _, _, faces = side_values(values[r], idx[2, 2], idx[2, 3], idx[2, 4])
        row = jnp.where(group == 0, south[0], north[CHUNKS - 1])
        for v in range(CHUNKS):
            use = (chunk_of_lane == v) & ((group == 1) | (group == 2))
            row = jnp.where(use, by_lane(faces[v], face_lane), row)
        packed[:PPD, 2 * PLANES + 4, r - 1, :] = row - level
    packed[PPD] = jnp.zeros_like(packed[PPD])

    def fill_slot(d, carry):
        sbuf[d] = packed[inv_ref[d]].astype(jnp.bfloat16)
        return carry

    lax.fori_loop(0, nz * ny, fill_slot, 0)

    def shift_of(i):
        def far_first(j, size):
            return size // 2 + (1 - 2 * lax.rem(j, 2)) * lax.div(j + 1, 2)

        a, b = lax.div(i - 1, ny), lax.rem(i - 1, ny)
        return far_first(lax.rem(a + b + 1, nz), nz), far_first(b, ny)

    def remap_copy(i):
        dz, dy = shift_of(i)
        there = lax.rem(z_me + dz, nz) * ny + lax.rem(y_me + dy, ny)
        return pltpu.make_async_remote_copy(
            src_ref=sbuf.at[there],
            dst_ref=rbuf.at[patch],
            send_sem=a_send.at[i],
            recv_sem=a_recv.at[i],
            device_id=(there, field),
            device_id_type=MESH,
        )

    def start_copy(i, carry):
        remap_copy(i).start()
        return carry

    lax.fori_loop(1, nz * ny, start_copy, 0)

    chunk = lax.broadcasted_iota(jnp.int32, (CHUNKS, LANES), 0)
    z = lane % SIDE
    spread_lane = jnp.where(z == 0, SIDE, 2 * SIDE) + chunk * 4 + lane // SIDE
    low_corner = (chunk == 0) & (lane < SIDE)
    high_corner = (chunk == CHUNKS - 1) & (lane >= LANES - SIDE)

    def spread_rows(half, s):
        for r in range(PLANES + 2):
            for part in range(2):
                turn[half, r, part * 4 : part * 4 + 4, :] = rbuf[s, 2 * r + part].astype(jnp.float32)

    def form_gradient(half, s):
        rows = [turn[half, r] for r in range(PLANES + 2)]
        faces = rbuf[s, 2 * PLANES + 4].astype(jnp.float32)
        for x in range(PLANES):
            center = rows[x + 1]
            face = jnp.broadcast_to(faces[x : x + 1, :], (CHUNKS, LANES))
            face_z = by_lane(face, spread_lane)
            up = pltpu.roll(center, SIDE, 1)
            down = pltpu.roll(center, LANES - SIDE, 1)
            south = jnp.where(lane < SIDE, pltpu.roll(up, 1, 0), up)
            south = jnp.where(low_corner, face, south)
            north = jnp.where(lane >= LANES - SIDE, pltpu.roll(down, CHUNKS - 1, 0), down)
            north = jnp.where(high_corner, face, north)
            below = jnp.where(z == 0, face_z, pltpu.roll(center, 1, 1))
            above = jnp.where(z == SIDE - 1, face_z, pltpu.roll(center, LANES - 1, 1))
            out_ref[s, 0, x] = (0.5 * (rows[x + 2] - rows[x])).astype(jnp.bfloat16)
            out_ref[s, 1, x] = (0.5 * (north - south)).astype(jnp.bfloat16)
            out_ref[s, 2, x] = (0.5 * (above - below)).astype(jnp.bfloat16)

    def finish(slots):
        for half, s in enumerate(slots):
            spread_rows(half, s)
        for half, s in enumerate(slots):
            form_gradient(half, s)

    def origin_of(i):
        dz, dy = shift_of(i)
        return lax.rem(z_me + nz - dz, nz) * ny + lax.rem(y_me + ny - dy, ny)

    rbuf[patch] = sbuf[patch]
    remap_copy(1).wait_recv()
    finish([patch, origin_of(1)])

    def take_pair(i, carry):
        remap_copy(2 * i).wait_recv()
        remap_copy(2 * i + 1).wait_recv()
        finish([origin_of(2 * i), origin_of(2 * i + 1)])
        return carry

    lax.fori_loop(1, nz * ny // 2, take_pair, 0)

    def end_copy(i, carry):
        remap_copy(i).wait_send()
        return carry

    for copy in x_copies + y_copies + z_copies:
        copy.wait_send()
    lax.fori_loop(1, nz * ny, end_copy, 0)


def on_device(pressure_start, divergence, neighbors, advect_slot, point_cell, point_force):
    n_patch = lax.axis_size("patch")
    nf = lax.axis_size("field")
    ny = math.isqrt(n_patch)
    nz = n_patch // ny
    cells = point_cell.reshape(n_patch, -1)
    if cells.shape[1] < LANES:
        cells = jnp.pad(cells, ((0, 0), (0, LANES - cells.shape[1])), constant_values=-1)

    far = pl.BlockSpec(memory_space=pltpu.HBM)
    dma = pltpu.SemaphoreType.DMA
    slot = (2 * PLANES + 5, 4, LANES)
    inputs = (advect_slot, point_force, pressure_start, divergence, neighbors, cells)
    return pl.pallas_call(
        functools.partial(step_kernel, nz, ny, nf),
        out_shape=jax.ShapeDtypeStruct((n_patch, 3, PLANES, CHUNKS, LANES), jnp.bfloat16),
        in_specs=[far, far, far, far, far, far],
        out_specs=pl.BlockSpec(memory_space=pltpu.VMEM),
        scratch_shapes=[
            pltpu.SMEM((n_patch,), jnp.int32),
            pltpu.VMEM((1, LANES), jnp.float32),
            pltpu.VMEM((n_patch, LANES), jnp.int32),
            pltpu.VMEM((n_patch,) + slot, jnp.bfloat16),
            pltpu.VMEM((2, PLANES + 2, CHUNKS, LANES), jnp.float32),
            pltpu.SMEM(advect_slot.shape, jnp.int32),
            pltpu.SMEM(point_force.shape, jnp.float32),
            pltpu.VMEM((SLABS, PLANES + 2, PPD, AREA), jnp.float32),
            pltpu.VMEM((SLABS, PLANES + 2, PPD, AREA), jnp.float32),
            pltpu.VMEM((SLABS, PLANES, PPD, AREA), jnp.float32),
            pltpu.VMEM((SLABS, PPD, 6), jnp.int32),
            pltpu.VMEM((nf, 1, LANES), jnp.float32),
            pltpu.VMEM((ny, 1, LANES), jnp.float32),
            pltpu.VMEM((nz, ny, 1, LANES), jnp.float32),
            pltpu.VMEM((nz, ROWS_HOT, ny * LANES), jnp.bfloat16),
            pltpu.VMEM((nz, 256, ny * LANES), jnp.bfloat16),
            pltpu.VMEM((256, ny * LANES), jnp.bfloat16),
            pltpu.VMEM((ROWS_HOT, 256), jnp.float32),
            pltpu.VMEM((SLABS, 5, PPD, LANES), jnp.int32),
            pltpu.VMEM((PPD + 1,) + slot, jnp.float32),
            pltpu.VMEM((n_patch,) + slot, jnp.bfloat16),
            dma((2, PLANES + 1)),
            dma((3, 4)),
            dma((3, 4)),
            dma((nf - 1,)),
            dma((nf - 1,)),
            dma((ny - 1,)),
            dma((ny - 1,)),
            dma((nz - 1,)),
            dma((nz - 1,)),
            dma((n_patch,)),
            dma((n_patch,)),
            dma((2,)),
        ],
        compiler_params=pltpu.CompilerParams(
            collective_id=0, has_side_effects=True, vmem_limit_bytes=48*1024*1024
        ),
        name="step",
    )(*[pltpu.with_memory_space_constraint(v, pltpu.HBM) for v in inputs]).reshape(n_patch, 3, PLANES, AREA)
def solution(mesh):
    in_specs = (
        P("patch", "field", None),
        P("patch", "field", None),
        P("patch", None),
        P("patch"),
        P(),
        P(("patch", "field")),
    )
    out_specs = P("patch", None, "field", None)
    return jax.shard_map(
        on_device, mesh=mesh, in_specs=in_specs, out_specs=out_specs, check_vma=False
    )
```

```python
import functools
import math

import jax
import jax.numpy as jnp
from jax import lax
from jax.experimental import pallas as pl
from jax.experimental.pallas import tpu as pltpu
from jax.sharding import PartitionSpec as P

SIDE = 32
SWEEPS = 6
PPD = 8
PLANES = 4
AREA = SIDE * SIDE
CHUNKS = AREA // 128
SLABS = 5
LANES = 128
REGION = 16
ROWS_HOT = REGION * PPD * (AREA // 256)
MESH = pl.DeviceIdType.MESH

relaxation = 1.0 / 9.0


def lane_iota():
    return lax.broadcasted_iota(jnp.int32, (PPD, LANES), 1)


def by_patch(value, index):
    return jnp.take_along_axis(value, index, axis=0, mode="promise_in_bounds")


def by_lane(value, index):
    return jnp.take_along_axis(value, index, axis=1, mode="promise_in_bounds")


def turned(chunks):
    group = lane_iota() // SIDE
    result = []
    for v in range(CHUNKS):
        parts = [
            pltpu.roll(chunks[2 * j + v // 4], SIDE * ((j - v) % 4), 1)
            if (j - v) % 4
            else chunks[2 * j + v // 4]
            for j in range(4)
        ]
        low = jnp.where(group == 0, parts[0], parts[1])
        high = jnp.where(group == 2, parts[2], parts[3])
        result.append(jnp.where(group < 2, low, high))
    return result


def turned_back(chunks):
    group = lane_iota() // SIDE
    result = []
    for c in range(CHUNKS):
        j, q = divmod(c, 2)
        parts = [
            pltpu.roll(chunks[4 * q + g], SIDE * ((g - j) % 4), 1)
            if (g - j) % 4
            else chunks[4 * q + g]
            for g in range(4)
        ]
        low = jnp.where(group == 0, parts[0], parts[1])
        high = jnp.where(group == 2, parts[2], parts[3])
        result.append(jnp.where(group < 2, low, high))
    return result


def along_z_values(center, idx_z):
    lane = lane_iota()
    z = lane % SIDE
    lower = jnp.where(z == 0, lane + (SIDE - 1), lane - 1)
    upper = jnp.where(z == SIDE - 1, lane - (SIDE - 1), lane + 1)
    below, above = [], []
    for c in center:
        mixed = by_patch(c, idx_z)
        below.append(by_lane(jnp.where(z == SIDE - 1, mixed, c), lower))
        above.append(by_lane(jnp.where(z == 0, mixed, c), upper))
    return below, above


def along_y_values(center, idx_south, idx_north):
    lane = lane_iota()
    up = pltpu.roll(center[CHUNKS - 1], SIDE, 1)
    down = pltpu.roll(center[0], LANES - SIDE, 1)
    first = jnp.where(lane < SIDE, by_patch(up, idx_south), up)
    last = jnp.where(lane >= LANES - SIDE, by_patch(down, idx_north), down)
    return [first] + center[:-1], center[1:] + [last]


def chunks_of(ref, k, row):
    return [ref[k, row, :, v * LANES : (v + 1) * LANES] for v in range(CHUNKS)]


def step_kernel(
    nz,
    ny,
    nf,
    adv_ref,
    force_ref,
    p_ref,
    d_ref,
    tab_ref,
    cell_ref,
    out_ref,
    inv_ref,
    frow_ref,
    pc_ref,
    rbuf,
    turn,
    held,
    adv_smem,
    force_smem,
    pa,
    pb,
    src,
    tabs,
    xbuf,
    ybuf,
    forces,
    hot_a,
    hot_b,
    scaled,
    acc,
    idx,
    packed,
    sbuf,
    load_sem,
    halo_send,
    halo_recv,
    x_send,
    x_recv,
    y_send,
    y_recv,
    z_send,
    z_recv,
    a_send,
    a_recv,
    out_sem,
):
    patch = lax.axis_index("patch")
    field = lax.axis_index("field")
    z_me = lax.div(patch, ny)
    y_me = lax.rem(patch, ny)
    total = nz * ny * nf
    line = patch * nf + field
    x_side = PLANES * nf

    def along_line(k):
        other = lax.rem(line + (k + total), total)
        return (lax.div(other, nf), lax.rem(other, nf))

    def along_x(k):
        return (patch, lax.rem(field + k, nf))

    def along_y(k):
        return (z_me * ny + lax.rem(y_me + k, ny), field)

    def along_z(k):
        return (lax.rem(z_me + k, nz) * ny + y_me, field)

    loads = []
    for x in range(PLANES):
        loads.append(
            pltpu.make_async_copy(p_ref.at[:, x, :], held.at[0, x], load_sem.at[0, x])
        )
        loads.append(pltpu.make_async_copy(d_ref.at[:, x, :], held.at[1, x], load_sem.at[1, x]))
    loads.append(pltpu.make_async_copy(tab_ref, tabs.at[2], load_sem.at[0, PLANES]))
    small = [
        pltpu.make_async_copy(force_ref, force_smem, out_sem.at[0]),
        pltpu.make_async_copy(adv_ref, adv_smem, out_sem.at[1]),
    ]
    for copy in small:
        copy.start()
    cells = pltpu.make_async_copy(cell_ref, pc_ref, load_sem.at[1, PLANES])
    cells.start()
    for copy in loads:
        copy.start()

    barrier = pltpu.get_barrier_semaphore()
    greeted = [along_x(k) for k in range(1, nf)]
    greeted += [along_y(k) for k in range(1, ny)]
    greeted += [along_z(k) for k in range(1, nz)]
    greeted += [along_line(k) for k in (1, -1, 2, -2)]
    for device in greeted:
        pl.semaphore_signal(barrier, inc=1, device_id=device, device_id_type=MESH)

    per_device = force_ref.shape[0]
    row_lane = lax.broadcasted_iota(jnp.int32, (1, LANES), 1) - per_device * field
    row = jnp.zeros((1, LANES), jnp.float32)
    for copy in small:
        copy.wait()
    for i in range(per_device):
        row = jnp.where(row_lane == i, force_smem[i], row)
    frow_ref[...] = row
    owners = [adv_smem[i] for i in range(PPD)]

    def find_patch(d, carry):
        found = jnp.int32(PPD)
        for i in range(PPD):
            found = jnp.where(owners[i] == d, jnp.int32(i), found)
        inv_ref[d] = found
        return carry


    base_rows = lax.broadcasted_iota(jnp.int32, (16, LANES), 0).astype(jnp.float32).astype(jnp.bfloat16)

    def build_hot(row, carry):
        zrow = lax.div(row, ny)
        yrow = lax.rem(row, ny)
        cell = pc_ref[pl.ds(row, 1), :]
        q = cell // (x_side * AREA)
        inside = cell % (x_side * AREA)
        plane = lax.div(q, PPD) * x_side + lax.div(inside, AREA)
        lp = lax.rem(q, PPD)
        natural = lax.rem(inside, AREA)
        y = lax.div(natural, SIDE)
        cell_in_plane = lax.rem(y, CHUNKS) * LANES + lax.div(y, CHUNKS) * SIDE + lax.rem(natural, SIDE)
        e = plane - (line * PLANES - 6)
        m = (lax.div(cell_in_plane, 256) * REGION + e) * PPD + lp
        m = jnp.where((e >= 0) & (e < REGION), m, -1)
        n = lax.rem(cell_in_plane, 256)
        lanes = pl.ds(pl.multiple_of(yrow * LANES, LANES), LANES)
        def one_hot(place, size):
            at = jnp.clip(place, -1, 256).astype(jnp.float32)
            at = jnp.broadcast_to(at, (16, LANES)).astype(jnp.bfloat16)
            one = jnp.ones((16, LANES), jnp.bfloat16)
            return [
                jnp.where(base_rows + jnp.bfloat16(16 * b) == at, one, one - one)
                for b in range(size // 16)
            ]

        for part in range(ROWS_HOT // 256):
            for b, block in enumerate(one_hot(m - 256 * part, 256)):
                hot_a[zrow, part * 256 + b * 16 : part * 256 + (b + 1) * 16, lanes] = block
        for b, block in enumerate(one_hot(n, 256)):
            hot_b[zrow, b * 16 : (b + 1) * 16, lanes] = block
        return carry

    cells.wait()
    lax.fori_loop(0, nz * ny // 4, build_hot, 0)
    pl.semaphore_wait(barrier, len(greeted))

    def send(source, target, s_sem, r_sem, device):
        copy = pltpu.make_async_remote_copy(
            src_ref=source,
            dst_ref=target,
            send_sem=s_sem,
            recv_sem=r_sem,
            device_id=device,
            device_id_type=MESH,
        )
        copy.start()
        return copy

    x_copies = [
        send(frow_ref, xbuf.at[field], x_send.at[k - 1], x_recv.at[k - 1], along_x(k))
        for k in range(1, nf)
    ]
    for copy in loads:
        copy.wait()
    for x in range(PLANES):
        for kind in range(2):
            chunks = turned(chunks_of(held, kind, x))
            for v in range(CHUNKS):
                lanes = slice(v * LANES, (v + 1) * LANES)
                if kind == 0:
                    pa[2, x + 1, :, lanes] = chunks[v]
                else:
                    src[2, x, :, lanes] = chunks[v]
    halo = []
    for i, (k, lo, hi, dlo, dhi) in enumerate(
        ((1, 0, 4, 0, 4), (-1, 0, 4, 0, 4), (2, 1, 4, 2, 4), (-2, 0, 3, 0, 2))
    ):
        there = along_line(k)
        slot = 2 - k
        halo.append(
            send(
                pa.at[2, lo + 1 : hi + 1],
                pa.at[slot, lo + 1 : hi + 1],
                halo_send.at[0, i],
                halo_recv.at[0, i],
                there,
            )
        )
        halo.append(
            send(
                src.at[2, dlo:dhi],
                src.at[slot, dlo:dhi],
                halo_send.at[1, i],
                halo_recv.at[1, i],
                there,
            )
        )
        halo.append(
            send(tabs.at[2], tabs.at[slot], halo_send.at[2, i], halo_recv.at[2, i], there)
        )

    half = nz * ny * 3 // 4
    lax.fori_loop(nz * ny // 4, half, build_hot, 0)

    for copy in x_copies:
        copy.wait_recv()
    row = frow_ref[...]
    for k in range(1, nf):
        row = row + xbuf[lax.rem(field + k, nf)]
    ybuf[y_me] = row
    y_copies = [
        send(ybuf.at[y_me], ybuf.at[y_me], y_send.at[k - 1], y_recv.at[k - 1], along_y(k))
        for k in range(1, ny)
    ]
    acc[...] = jnp.zeros_like(acc)
    lax.fori_loop(half, nz * ny, build_hot, 0)
    lax.fori_loop(0, nz * ny, find_patch, 0)
    for copy in y_copies:
        copy.wait_recv()
    z_copies = [
        send(ybuf, forces.at[z_me], z_send.at[k - 1], z_recv.at[k - 1], along_z(k))
        for k in range(1, nz)
    ]
    forces[z_me] = ybuf[...]

    def add_points(zrow):
        for yrow in range(ny):
            lanes = slice(yrow * LANES, (yrow + 1) * LANES)
            wide = jnp.broadcast_to(forces[zrow, yrow], (16, LANES)).astype(jnp.bfloat16)
            for b in range(16):
                rows = slice(b * 16, (b + 1) * 16)
                scaled[rows, lanes] = hot_b[zrow, rows, lanes] * wide
        acc[...] += lax.dot_general(
            hot_a[zrow],
            scaled[...],
            (((1,), (1,)), ((), ())),
            preferred_element_type=jnp.float32,
        )

    add_points(z_me)

    for copy in halo:
        copy.wait_recv()
    zero_idx = jnp.zeros((PPD, LANES), jnp.int32)
    own_row = lax.broadcasted_iota(jnp.int32, (PPD, LANES), 0)
    z_lane = lane_iota() % SIDE
    for k in range(SLABS):
        table = tabs[k]
        columns = [zero_idx + table[:, c : c + 1] for c in range(6)]
        fk = lax.rem(field + (k - 2 + nf), nf)
        idx[k, 0] = jnp.where(fk == 0, columns[0], own_row)
        idx[k, 1] = jnp.where(fk == nf - 1, columns[1], own_row)
        idx[k, 2] = columns[2] & (PPD - 1)
        idx[k, 3] = columns[3] & (PPD - 1)
        idx[k, 4] = jnp.where(z_lane == 0, columns[5], columns[4]) & (PPD - 1)

    def fill_ghosts(ref, edges):
        for k in edges:
            west, east = idx[k, 0], idx[k - 1, 1]
            west_values = chunks_of(ref, k - 1, PLANES)
            east_values = chunks_of(ref, k, 1)
            for v in range(CHUNKS):
                lanes = slice(v * LANES, (v + 1) * LANES)
                ref[k, 0, :, lanes] = jnp.where(
                    west >= 0, by_patch(west_values[v], west & (PPD - 1)), 0.0
                )
                ref[k - 1, PLANES + 1, :, lanes] = jnp.where(
                    east >= 0, by_patch(east_values[v], east & (PPD - 1)), 0.0
                )

    def sweep(old, new, lo, hi):
        def relax(g):
            k = lax.div(g, PLANES)
            j = lax.rem(g, PLANES)
            west = chunks_of(old, k, j)
            center = chunks_of(old, k, j + 1)
            east = chunks_of(old, k, j + 2)
            south, north = along_y_values(center, idx[k, 2], idx[k, 3])
            below, above = along_z_values(center, idx[k, 4])
            result = []
            for v in range(CHUNKS):
                around = west[v] + east[v] + south[v] + north[v] + below[v] + above[v]
                source = src[k, j, :, v * LANES : (v + 1) * LANES]
                result.append(center[v] + relaxation * (source - (6.0 * center[v] - around)))
            return k, j, result

        def body(i, carry):
            done = [relax(lo + 2 * i), relax(lo + 2 * i + 1)]
            for k, j, result in done:
                for v in range(CHUNKS):
                    new[k, j + 1, :, v * LANES : (v + 1) * LANES] = result[v]
            return carry

        lax.fori_loop(0, (hi + 1 - lo) // 2, body, 0)

    fill_ghosts(pa, range(1, SLABS))
    for copy in halo:
        copy.wait_send()
    sweep(pa, pb, 2, 17)

    for k in sorted(range(1, nz), key=lambda k: min(k, nz - k)):
        z_copies[k - 1].wait_recv()
        add_points(lax.rem(z_me + (nz - k), nz))

    for e in range(REGION):
        k, j = divmod(e + 2, PLANES)
        for part in range(AREA // 256):
            extra = acc[(part * REGION + e) * PPD : (part * REGION + e + 1) * PPD, :]
            lanes = slice(part * 256, (part + 1) * 256)
            src[k, j, :, lanes] += extra
            pb[k, j + 1, :, lanes] += relaxation * extra

    refs = (pa, pb)
    for t in range(2, SWEEPS + 1):
        old, new = refs[(t + 1) % 2], refs[t % 2]
        reach = SWEEPS - t
        fill_ghosts(old, range(1, SLABS) if reach >= 1 else (2, 3))
        sweep(old, new, 7 - reach, 12 + reach)
    final = refs[SWEEPS % 2]
    fill_ghosts(final, (2, 3))

    ghosts = [chunks_of(final, 2, r) for r in range(PLANES + 2)]
    values = [turned_back(chunks) for chunks in ghosts]
    level = values[1][0]
    for r in range(1, PLANES + 1):
        for v in range(CHUNKS):
            if (r, v) != (1, 0):
                level = level + values[r][v]
    level = jnp.sum(level, axis=1, keepdims=True) * (1.0 / (PLANES * AREA))
    lane = lane_iota()
    group = lane // SIDE
    within = lane % SIDE
    chunk_of_lane = within // 4
    within_z = lane % SIDE
    face_lane = (within % 4) * SIDE + jnp.where(group == 2, SIDE - 1, 0)
    for r in range(PLANES + 2):
        for v in range(CHUNKS):
            packed[:PPD, 2 * r + v // 4, v % 4, :] = values[r][v] - level
    for r in range(1, PLANES + 1):
        south, north = along_y_values(ghosts[r], idx[2, 2], idx[2, 3])
        below, above = along_z_values(values[r], idx[2, 4])
        row = jnp.where(group == 0, south[0], north[CHUNKS - 1])
        for v in range(CHUNKS):
            use = (chunk_of_lane == v) & ((group == 1) | (group == 2))
            faces = jnp.where(within_z == 0, below[v], above[v])
            row = jnp.where(use, by_lane(faces, face_lane), row)
        packed[:PPD, 2 * PLANES + 4, r - 1, :] = row - level
    packed[PPD] = jnp.zeros_like(packed[PPD])

    def fill_slot(d):
        sbuf[d] = packed[inv_ref[d]].astype(jnp.bfloat16)

    def shift_of(i):
        def far_first(j, size):
            return size // 2 + (1 - 2 * lax.rem(j, 2)) * lax.div(j + 1, 2)

        a, b = lax.div(i - 1, ny), lax.rem(i - 1, ny)
        return far_first(lax.rem(a + b + 1, nz), nz), far_first(b, ny)

    def target_of(i):
        dz, dy = shift_of(i)
        return lax.rem(z_me + dz, nz) * ny + lax.rem(y_me + dy, ny)

    def remap_copy(i):
        there = target_of(i)
        return pltpu.make_async_remote_copy(
            src_ref=sbuf.at[there],
            dst_ref=rbuf.at[patch],
            send_sem=a_send.at[i],
            recv_sem=a_recv.at[i],
            device_id=(there, field),
            device_id_type=MESH,
        )

    ahead = 3

    def start_copies(i, carry):
        first = 1 + ahead * i
        for k in range(ahead):
            fill_slot(target_of(first + ahead + k))
        for k in range(ahead):
            remap_copy(first + k).start()
        return carry

    rounds = (nz * ny - 1) // ahead
    for k in range(1, ahead + 1):
        fill_slot(target_of(k))
    lax.fori_loop(0, rounds - 1, start_copies, 0)
    for k in range(nz * ny - ahead, nz * ny):
        remap_copy(k).start()
    fill_slot(patch)

    chunk = lax.broadcasted_iota(jnp.int32, (CHUNKS, LANES), 0)
    z = lane % SIDE
    spread_lane = jnp.where(z == 0, SIDE, 2 * SIDE) + chunk * 4 + lane // SIDE
    low_corner = (chunk == 0) & (lane < SIDE)
    high_corner = (chunk == CHUNKS - 1) & (lane >= LANES - SIDE)

    def spread_rows(half, s):
        for r in range(PLANES + 2):
            for part in range(2):
                turn[half, r, part * 4 : part * 4 + 4, :] = rbuf[s, 2 * r + part].astype(jnp.float32)

    def form_gradient(half, s):
        rows = [turn[half, r] for r in range(PLANES + 2)]
        faces = rbuf[s, 2 * PLANES + 4].astype(jnp.float32)
        for x in range(PLANES):
            center = rows[x + 1]
            face = jnp.broadcast_to(faces[x : x + 1, :], (CHUNKS, LANES))
            face_z = by_lane(face, spread_lane)
            up = pltpu.roll(center, SIDE, 1)
            down = pltpu.roll(center, LANES - SIDE, 1)
            south = jnp.where(lane < SIDE, pltpu.roll(up, 1, 0), up)
            south = jnp.where(low_corner, face, south)
            north = jnp.where(lane >= LANES - SIDE, pltpu.roll(down, CHUNKS - 1, 0), down)
            north = jnp.where(high_corner, face, north)
            below = jnp.where(z == 0, face_z, pltpu.roll(center, 1, 1))
            above = jnp.where(z == SIDE - 1, face_z, pltpu.roll(center, LANES - 1, 1))
            out_ref[s, 0, x] = (0.5 * (rows[x + 2] - rows[x])).astype(jnp.bfloat16)
            out_ref[s, 1, x] = (0.5 * (north - south)).astype(jnp.bfloat16)
            out_ref[s, 2, x] = (0.5 * (above - below)).astype(jnp.bfloat16)

    def finish(slots):
        for half, s in enumerate(slots):
            spread_rows(half, s)
        for half, s in enumerate(slots):
            form_gradient(half, s)

    def origin_of(i):
        dz, dy = shift_of(i)
        return lax.rem(z_me + nz - dz, nz) * ny + lax.rem(y_me + ny - dy, ny)

    rbuf[patch] = sbuf[patch]
    remap_copy(1).wait_recv()
    finish([patch, origin_of(1)])

    def take_pair(i, carry):
        remap_copy(2 * i).wait_recv()
        remap_copy(2 * i + 1).wait_recv()
        finish([origin_of(2 * i), origin_of(2 * i + 1)])
        return carry

    lax.fori_loop(1, nz * ny // 2, take_pair, 0)

    def end_copy(i, carry):
        remap_copy(i).wait_send()
        return carry

    for copy in x_copies + y_copies + z_copies:
        copy.wait_send()
    lax.fori_loop(1, nz * ny, end_copy, 0)


def on_device(pressure_start, divergence, neighbors, advect_slot, point_cell, point_force):
    n_patch = lax.axis_size("patch")
    nf = lax.axis_size("field")
    ny = math.isqrt(n_patch)
    nz = n_patch // ny
    cells = point_cell.reshape(n_patch, -1)
    if cells.shape[1] < LANES:
        cells = jnp.pad(cells, ((0, 0), (0, LANES - cells.shape[1])), constant_values=-1)

    far = pl.BlockSpec(memory_space=pltpu.HBM)
    dma = pltpu.SemaphoreType.DMA
    slot = (2 * PLANES + 5, 4, LANES)
    inputs = (advect_slot, point_force, pressure_start, divergence, neighbors, cells)
    return pl.pallas_call(
        functools.partial(step_kernel, nz, ny, nf),
        out_shape=jax.ShapeDtypeStruct((n_patch, 3, PLANES, CHUNKS, LANES), jnp.bfloat16),
        in_specs=[far, far, far, far, far, far],
        out_specs=pl.BlockSpec(memory_space=pltpu.VMEM),
        scratch_shapes=[
            pltpu.SMEM((n_patch,), jnp.int32),
            pltpu.VMEM((1, LANES), jnp.float32),
            pltpu.VMEM((n_patch, LANES), jnp.int32),
            pltpu.VMEM((n_patch,) + slot, jnp.bfloat16),
            pltpu.VMEM((2, PLANES + 2, CHUNKS, LANES), jnp.float32),
            pltpu.VMEM((2, PLANES, PPD, AREA), jnp.float32),
            pltpu.SMEM(advect_slot.shape, jnp.int32),
            pltpu.SMEM(point_force.shape, jnp.float32),
            pltpu.VMEM((SLABS, PLANES + 2, PPD, AREA), jnp.float32),
            pltpu.VMEM((SLABS, PLANES + 2, PPD, AREA), jnp.float32),
            pltpu.VMEM((SLABS, PLANES, PPD, AREA), jnp.float32),
            pltpu.VMEM((SLABS, PPD, 6), jnp.int32),
            pltpu.VMEM((nf, 1, LANES), jnp.float32),
            pltpu.VMEM((ny, 1, LANES), jnp.float32),
            pltpu.VMEM((nz, ny, 1, LANES), jnp.float32),
            pltpu.VMEM((nz, ROWS_HOT, ny * LANES), jnp.bfloat16),
            pltpu.VMEM((nz, 256, ny * LANES), jnp.bfloat16),
            pltpu.VMEM((256, ny * LANES), jnp.bfloat16),
            pltpu.VMEM((ROWS_HOT, 256), jnp.float32),
            pltpu.VMEM((SLABS, 5, PPD, LANES), jnp.int32),
            pltpu.VMEM((PPD + 1,) + slot, jnp.float32),
            pltpu.VMEM((n_patch,) + slot, jnp.bfloat16),
            dma((2, PLANES + 1)),
            dma((3, 4)),
            dma((3, 4)),
            dma((nf - 1,)),
            dma((nf - 1,)),
            dma((ny - 1,)),
            dma((ny - 1,)),
            dma((nz - 1,)),
            dma((nz - 1,)),
            dma((n_patch,)),
            dma((n_patch,)),
            dma((2,)),
        ],
        compiler_params=pltpu.CompilerParams(
            collective_id=0, has_side_effects=True, vmem_limit_bytes=48*1024*1024
        ),
        name="step",
    )(*[pltpu.with_memory_space_constraint(v, pltpu.HBM) for v in inputs]).reshape(n_patch, 3, PLANES, AREA)
def solution(mesh):
    in_specs = (
        P("patch", "field", None),
        P("patch", "field", None),
        P("patch", None),
        P("patch"),
        P(),
        P(("patch", "field")),
    )
    out_specs = P("patch", None, "field", None)
    return jax.shard_map(
        on_device, mesh=mesh, in_specs=in_specs, out_specs=out_specs, check_vma=False
    )
```

```python
import functools
import math

import jax
import jax.numpy as jnp
from jax import lax
from jax.experimental import pallas as pl
from jax.experimental.pallas import tpu as pltpu
from jax.sharding import PartitionSpec as P

SIDE = 32
SWEEPS = 6
PPD = 8
PLANES = 4
AREA = SIDE * SIDE
CHUNKS = AREA // 128
SLABS = 5
LANES = 128
REGION = 16
ROWS_HOT = REGION * PPD * (AREA // 256)
MESH = pl.DeviceIdType.MESH

relaxation = 1.0 / 9.0


def lane_iota():
    return lax.broadcasted_iota(jnp.int32, (PPD, LANES), 1)


def by_patch(value, index):
    return jnp.take_along_axis(value, index, axis=0, mode="promise_in_bounds")


def by_lane(value, index):
    return jnp.take_along_axis(value, index, axis=1, mode="promise_in_bounds")


def turned(chunks):
    group = lane_iota() // SIDE
    result = []
    for v in range(CHUNKS):
        parts = [
            pltpu.roll(chunks[2 * j + v // 4], SIDE * ((j - v) % 4), 1)
            if (j - v) % 4
            else chunks[2 * j + v // 4]
            for j in range(4)
        ]
        low = jnp.where(group == 0, parts[0], parts[1])
        high = jnp.where(group == 2, parts[2], parts[3])
        result.append(jnp.where(group < 2, low, high))
    return result


def turned_back(chunks):
    group = lane_iota() // SIDE
    result = []
    for c in range(CHUNKS):
        j, q = divmod(c, 2)
        parts = [
            pltpu.roll(chunks[4 * q + g], SIDE * ((g - j) % 4), 1)
            if (g - j) % 4
            else chunks[4 * q + g]
            for g in range(4)
        ]
        low = jnp.where(group == 0, parts[0], parts[1])
        high = jnp.where(group == 2, parts[2], parts[3])
        result.append(jnp.where(group < 2, low, high))
    return result


def along_z_values(center, idx_z):
    lane = lane_iota()
    z = lane % SIDE
    lower = jnp.where(z == 0, lane + (SIDE - 1), lane - 1)
    upper = jnp.where(z == SIDE - 1, lane - (SIDE - 1), lane + 1)
    below, above = [], []
    for c in center:
        mixed = by_patch(c, idx_z)
        below.append(by_lane(jnp.where(z == SIDE - 1, mixed, c), lower))
        above.append(by_lane(jnp.where(z == 0, mixed, c), upper))
    return below, above


def along_y_values(center, idx_south, idx_north):
    lane = lane_iota()
    up = pltpu.roll(center[CHUNKS - 1], SIDE, 1)
    down = pltpu.roll(center[0], LANES - SIDE, 1)
    first = jnp.where(lane < SIDE, by_patch(up, idx_south), up)
    last = jnp.where(lane >= LANES - SIDE, by_patch(down, idx_north), down)
    return [first] + center[:-1], center[1:] + [last]


def chunks_of(ref, k, row):
    return [ref[k, row, :, v * LANES : (v + 1) * LANES] for v in range(CHUNKS)]


def step_kernel(
    nz,
    ny,
    nf,
    adv_ref,
    force_ref,
    p_ref,
    d_ref,
    tab_ref,
    cell_ref,
    out_ref,
    inv_ref,
    frow_ref,
    pc_ref,
    rbuf,
    turn,
    held,
    adv_smem,
    force_smem,
    pa,
    pb,
    src,
    tabs,
    xbuf,
    ybuf,
    forces,
    hot_a,
    hot_b,
    scaled,
    acc,
    idx,
    packed,
    sbuf,
    load_sem,
    halo_send,
    halo_recv,
    x_send,
    x_recv,
    y_send,
    y_recv,
    z_send,
    z_recv,
    a_send,
    a_recv,
    out_sem,
):
    patch = lax.axis_index("patch")
    field = lax.axis_index("field")
    z_me = lax.div(patch, ny)
    y_me = lax.rem(patch, ny)
    total = nz * ny * nf
    line = patch * nf + field
    x_side = PLANES * nf

    def along_line(k):
        other = lax.rem(line + (k + total), total)
        return (lax.div(other, nf), lax.rem(other, nf))

    def along_x(k):
        return (patch, lax.rem(field + k, nf))

    def along_y(k):
        return (z_me * ny + lax.rem(y_me + k, ny), field)

    def along_z(k):
        return (lax.rem(z_me + k, nz) * ny + y_me, field)

    loads = []
    for x in range(PLANES):
        loads.append(
            pltpu.make_async_copy(p_ref.at[:, x, :], held.at[0, x], load_sem.at[0, x])
        )
        loads.append(pltpu.make_async_copy(d_ref.at[:, x, :], held.at[1, x], load_sem.at[1, x]))
    loads.append(pltpu.make_async_copy(tab_ref, tabs.at[2], load_sem.at[0, PLANES]))
    small = [
        pltpu.make_async_copy(force_ref, force_smem, out_sem.at[0]),
        pltpu.make_async_copy(adv_ref, adv_smem, out_sem.at[1]),
    ]
    for copy in small:
        copy.start()
    cells = pltpu.make_async_copy(cell_ref, pc_ref, load_sem.at[1, PLANES])
    cells.start()
    for copy in loads:
        copy.start()

    barrier = pltpu.get_barrier_semaphore()
    greeted = [along_x(k) for k in range(1, nf)]
    greeted += [along_y(k) for k in range(1, ny)]
    greeted += [along_z(k) for k in range(1, nz)]
    greeted += [along_line(k) for k in (1, -1, 2, -2)]
    for device in greeted:
        pl.semaphore_signal(barrier, inc=1, device_id=device, device_id_type=MESH)

    per_device = force_ref.shape[0]
    row_lane = lax.broadcasted_iota(jnp.int32, (1, LANES), 1) - per_device * field
    row = jnp.zeros((1, LANES), jnp.float32)
    for copy in small:
        copy.wait()
    for i in range(per_device):
        row = jnp.where(row_lane == i, force_smem[i], row)
    frow_ref[...] = row
    owners = [adv_smem[i] for i in range(PPD)]

    def find_patch(d, carry):
        found = jnp.int32(PPD)
        for i in range(PPD):
            found = jnp.where(owners[i] == d, jnp.int32(i), found)
        inv_ref[d] = found
        return carry


    base_rows = lax.broadcasted_iota(jnp.int32, (16, LANES), 0).astype(jnp.float32).astype(jnp.bfloat16)

    def build_hot(row, carry):
        zrow = lax.div(row, ny)
        yrow = lax.rem(row, ny)
        cell = pc_ref[pl.ds(row, 1), :]
        q = cell // (x_side * AREA)
        inside = cell % (x_side * AREA)
        plane = lax.div(q, PPD) * x_side + lax.div(inside, AREA)
        lp = lax.rem(q, PPD)
        natural = lax.rem(inside, AREA)
        y = lax.div(natural, SIDE)
        cell_in_plane = lax.rem(y, CHUNKS) * LANES + lax.div(y, CHUNKS) * SIDE + lax.rem(natural, SIDE)
        e = plane - (line * PLANES - 6)
        m = (lax.div(cell_in_plane, 256) * REGION + e) * PPD + lp
        m = jnp.where((e >= 0) & (e < REGION), m, -1)
        n = lax.rem(cell_in_plane, 256)
        lanes = pl.ds(pl.multiple_of(yrow * LANES, LANES), LANES)
        def one_hot(place, size):
            at = jnp.clip(place, -1, 256).astype(jnp.float32)
            at = jnp.broadcast_to(at, (16, LANES)).astype(jnp.bfloat16)
            one = jnp.ones((16, LANES), jnp.bfloat16)
            return [
                jnp.where(base_rows + jnp.bfloat16(16 * b) == at, one, one - one)
                for b in range(size // 16)
            ]

        for part in range(ROWS_HOT // 256):
            for b, block in enumerate(one_hot(m - 256 * part, 256)):
                hot_a[zrow, part * 256 + b * 16 : part * 256 + (b + 1) * 16, lanes] = block
        for b, block in enumerate(one_hot(n, 256)):
            hot_b[zrow, b * 16 : (b + 1) * 16, lanes] = block
        return carry

    cells.wait()
    lax.fori_loop(0, nz * ny // 4, build_hot, 0)
    pl.semaphore_wait(barrier, len(greeted))

    def send(source, target, s_sem, r_sem, device):
        copy = pltpu.make_async_remote_copy(
            src_ref=source,
            dst_ref=target,
            send_sem=s_sem,
            recv_sem=r_sem,
            device_id=device,
            device_id_type=MESH,
        )
        copy.start()
        return copy

    x_copies = [
        send(frow_ref, xbuf.at[field], x_send.at[k - 1], x_recv.at[k - 1], along_x(k))
        for k in range(1, nf)
    ]
    for copy in loads:
        copy.wait()
    for x in range(PLANES):
        for kind in range(2):
            chunks = turned(chunks_of(held, kind, x))
            for v in range(CHUNKS):
                lanes = slice(v * LANES, (v + 1) * LANES)
                if kind == 0:
                    pa[2, x + 1, :, lanes] = chunks[v]
                else:
                    src[2, x, :, lanes] = chunks[v]
    halo = []
    for i, (k, lo, hi, dlo, dhi) in enumerate(
        ((1, 0, 4, 0, 4), (-1, 0, 4, 0, 4), (2, 1, 4, 2, 4), (-2, 0, 3, 0, 2))
    ):
        there = along_line(k)
        slot = 2 - k
        halo.append(
            send(
                pa.at[2, lo + 1 : hi + 1],
                pa.at[slot, lo + 1 : hi + 1],
                halo_send.at[0, i],
                halo_recv.at[0, i],
                there,
            )
        )
        halo.append(
            send(
                src.at[2, dlo:dhi],
                src.at[slot, dlo:dhi],
                halo_send.at[1, i],
                halo_recv.at[1, i],
                there,
            )
        )
        halo.append(
            send(tabs.at[2], tabs.at[slot], halo_send.at[2, i], halo_recv.at[2, i], there)
        )

    half = nz * ny * 3 // 4
    lax.fori_loop(nz * ny // 4, half, build_hot, 0)

    for copy in x_copies:
        copy.wait_recv()
    row = frow_ref[...]
    for k in range(1, nf):
        row = row + xbuf[lax.rem(field + k, nf)]
    ybuf[y_me] = row
    y_copies = [
        send(ybuf.at[y_me], ybuf.at[y_me], y_send.at[k - 1], y_recv.at[k - 1], along_y(k))
        for k in range(1, ny)
    ]
    acc[...] = jnp.zeros_like(acc)
    lax.fori_loop(half, nz * ny, build_hot, 0)
    lax.fori_loop(0, nz * ny, find_patch, 0)
    for copy in y_copies:
        copy.wait_recv()
    z_copies = [
        send(ybuf, forces.at[z_me], z_send.at[k - 1], z_recv.at[k - 1], along_z(k))
        for k in range(1, nz)
    ]
    forces[z_me] = ybuf[...]

    def add_points(zrow):
        for yrow in range(ny):
            lanes = slice(yrow * LANES, (yrow + 1) * LANES)
            wide = jnp.broadcast_to(forces[zrow, yrow], (16, LANES)).astype(jnp.bfloat16)
            for b in range(16):
                rows = slice(b * 16, (b + 1) * 16)
                scaled[rows, lanes] = hot_b[zrow, rows, lanes] * wide
        acc[...] += lax.dot_general(
            hot_a[zrow],
            scaled[...],
            (((1,), (1,)), ((), ())),
            preferred_element_type=jnp.float32,
        )

    add_points(z_me)

    for copy in halo:
        copy.wait_recv()
    zero_idx = jnp.zeros((PPD, LANES), jnp.int32)
    own_row = lax.broadcasted_iota(jnp.int32, (PPD, LANES), 0)
    z_lane = lane_iota() % SIDE
    for k in range(SLABS):
        table = tabs[k]
        columns = [zero_idx + table[:, c : c + 1] for c in range(6)]
        fk = lax.rem(field + (k - 2 + nf), nf)
        idx[k, 0] = jnp.where(fk == 0, columns[0], own_row)
        idx[k, 1] = jnp.where(fk == nf - 1, columns[1], own_row)
        idx[k, 2] = columns[2] & (PPD - 1)
        idx[k, 3] = columns[3] & (PPD - 1)
        idx[k, 4] = jnp.where(z_lane == 0, columns[5], columns[4]) & (PPD - 1)

    def fill_ghosts(ref, edges):
        for k in edges:
            west, east = idx[k, 0], idx[k - 1, 1]
            west_values = chunks_of(ref, k - 1, PLANES)
            east_values = chunks_of(ref, k, 1)
            for v in range(CHUNKS):
                lanes = slice(v * LANES, (v + 1) * LANES)
                ref[k, 0, :, lanes] = jnp.where(
                    west >= 0, by_patch(west_values[v], west & (PPD - 1)), 0.0
                )
                ref[k - 1, PLANES + 1, :, lanes] = jnp.where(
                    east >= 0, by_patch(east_values[v], east & (PPD - 1)), 0.0
                )

    def sweep(old, new, lo, hi):
        def relax(g):
            k = lax.div(g, PLANES)
            j = lax.rem(g, PLANES)
            west = chunks_of(old, k, j)
            center = chunks_of(old, k, j + 1)
            east = chunks_of(old, k, j + 2)
            south, north = along_y_values(center, idx[k, 2], idx[k, 3])
            below, above = along_z_values(center, idx[k, 4])
            result = []
            for v in range(CHUNKS):
                around = west[v] + east[v] + south[v] + north[v] + below[v] + above[v]
                source = src[k, j, :, v * LANES : (v + 1) * LANES]
                result.append(center[v] + relaxation * (source - (6.0 * center[v] - around)))
            return k, j, result

        def body(i, carry):
            done = [relax(lo + 2 * i), relax(lo + 2 * i + 1)]
            for k, j, result in done:
                for v in range(CHUNKS):
                    new[k, j + 1, :, v * LANES : (v + 1) * LANES] = result[v]
            return carry

        lax.fori_loop(0, (hi + 1 - lo) // 2, body, 0)

    fill_ghosts(pa, range(1, SLABS))
    for copy in halo:
        copy.wait_send()
    sweep(pa, pb, 2, 17)

    for k in sorted(range(1, nz), key=lambda k: min(k, nz - k)):
        z_copies[k - 1].wait_recv()
        add_points(lax.rem(z_me + (nz - k), nz))

    for e in range(REGION):
        k, j = divmod(e + 2, PLANES)
        for part in range(AREA // 256):
            extra = acc[(part * REGION + e) * PPD : (part * REGION + e + 1) * PPD, :]
            lanes = slice(part * 256, (part + 1) * 256)
            src[k, j, :, lanes] += extra
            pb[k, j + 1, :, lanes] += relaxation * extra

    refs = (pa, pb)
    for t in range(2, SWEEPS + 1):
        old, new = refs[(t + 1) % 2], refs[t % 2]
        reach = SWEEPS - t
        fill_ghosts(old, range(1, SLABS) if reach >= 1 else (2, 3))
        sweep(old, new, 7 - reach, 12 + reach)
    final = refs[SWEEPS % 2]
    fill_ghosts(final, (2, 3))

    ghosts = [chunks_of(final, 2, r) for r in range(PLANES + 2)]
    values = [turned_back(chunks) for chunks in ghosts]
    level = values[1][0]
    for r in range(1, PLANES + 1):
        for v in range(CHUNKS):
            if (r, v) != (1, 0):
                level = level + values[r][v]
    level = jnp.sum(level, axis=1, keepdims=True) * (1.0 / (PLANES * AREA))
    lane = lane_iota()
    group = lane // SIDE
    within = lane % SIDE
    chunk_of_lane = within // 4
    within_z = lane % SIDE
    face_lane = (within % 4) * SIDE + jnp.where(group == 2, SIDE - 1, 0)
    for r in range(PLANES + 2):
        for v in range(CHUNKS):
            packed[:PPD, 2 * r + v // 4, v % 4, :] = values[r][v] - level
    for r in range(1, PLANES + 1):
        south, north = along_y_values(ghosts[r], idx[2, 2], idx[2, 3])
        below, above = along_z_values(values[r], idx[2, 4])
        row = jnp.where(group == 0, south[0], north[CHUNKS - 1])
        for v in range(CHUNKS):
            use = (chunk_of_lane == v) & ((group == 1) | (group == 2))
            faces = jnp.where(within_z == 0, below[v], above[v])
            row = jnp.where(use, by_lane(faces, face_lane), row)
        packed[:PPD, 2 * PLANES + 4, r - 1, :] = row - level
    packed[PPD] = jnp.zeros_like(packed[PPD])

    def fill_slot(d):
        sbuf[d] = packed[inv_ref[d]].astype(jnp.bfloat16)

    def shift_of(i):
        def far_first(j, size):
            return size // 2 + (1 - 2 * lax.rem(j, 2)) * lax.div(j + 1, 2)

        a, b = lax.div(i - 1, ny), lax.rem(i - 1, ny)
        return far_first(lax.rem(a + 3 * b + 3, nz), nz), far_first(b, ny)

    def target_of(i):
        dz, dy = shift_of(i)
        return lax.rem(z_me + dz, nz) * ny + lax.rem(y_me + dy, ny)

    def remap_copy(i):
        there = target_of(i)
        return pltpu.make_async_remote_copy(
            src_ref=sbuf.at[there],
            dst_ref=rbuf.at[patch],
            send_sem=a_send.at[i],
            recv_sem=a_recv.at[i],
            device_id=(there, field),
            device_id_type=MESH,
        )

    ahead = 3

    def start_copies(i, carry):
        first = 1 + ahead * i
        for k in range(ahead):
            fill_slot(target_of(first + ahead + k))
        for k in range(ahead):
            remap_copy(first + k).start()
        return carry

    rounds = (nz * ny - 1) // ahead
    for k in range(1, ahead + 1):
        fill_slot(target_of(k))
    lax.fori_loop(0, rounds - 1, start_copies, 0)
    for k in range(nz * ny - ahead, nz * ny):
        remap_copy(k).start()
    fill_slot(patch)

    chunk = lax.broadcasted_iota(jnp.int32, (CHUNKS, LANES), 0)
    z = lane % SIDE
    spread_lane = jnp.where(z == 0, SIDE, 2 * SIDE) + chunk * 4 + lane // SIDE
    low_corner = (chunk == 0) & (lane < SIDE)
    high_corner = (chunk == CHUNKS - 1) & (lane >= LANES - SIDE)

    def spread_rows(half, s):
        for r in range(PLANES + 2):
            for part in range(2):
                turn[half, r, part * 4 : part * 4 + 4, :] = rbuf[s, 2 * r + part].astype(jnp.float32)

    def form_gradient(half, s):
        rows = [turn[half, r] for r in range(PLANES + 2)]
        faces = rbuf[s, 2 * PLANES + 4].astype(jnp.float32)
        for x in range(PLANES):
            center = rows[x + 1]
            face = jnp.broadcast_to(faces[x : x + 1, :], (CHUNKS, LANES))
            face_z = by_lane(face, spread_lane)
            up = pltpu.roll(center, SIDE, 1)
            down = pltpu.roll(center, LANES - SIDE, 1)
            south = jnp.where(lane < SIDE, pltpu.roll(up, 1, 0), up)
            south = jnp.where(low_corner, face, south)
            north = jnp.where(lane >= LANES - SIDE, pltpu.roll(down, CHUNKS - 1, 0), down)
            north = jnp.where(high_corner, face, north)
            below = jnp.where(z == 0, face_z, pltpu.roll(center, 1, 1))
            above = jnp.where(z == SIDE - 1, face_z, pltpu.roll(center, LANES - 1, 1))
            out_ref[s, 0, x] = (0.5 * (rows[x + 2] - rows[x])).astype(jnp.bfloat16)
            out_ref[s, 1, x] = (0.5 * (north - south)).astype(jnp.bfloat16)
            out_ref[s, 2, x] = (0.5 * (above - below)).astype(jnp.bfloat16)

    def finish(slots):
        for half, s in enumerate(slots):
            spread_rows(half, s)
        for half, s in enumerate(slots):
            form_gradient(half, s)

    def origin_of(i):
        dz, dy = shift_of(i)
        return lax.rem(z_me + nz - dz, nz) * ny + lax.rem(y_me + ny - dy, ny)

    rbuf[patch] = sbuf[patch]
    remap_copy(1).wait_recv()
    finish([patch, origin_of(1)])

    def take_pair(i, carry):
        remap_copy(2 * i).wait_recv()
        remap_copy(2 * i + 1).wait_recv()
        finish([origin_of(2 * i), origin_of(2 * i + 1)])
        return carry

    lax.fori_loop(1, nz * ny // 2, take_pair, 0)

    def end_copy(i, carry):
        remap_copy(i).wait_send()
        return carry

    for copy in x_copies + y_copies + z_copies:
        copy.wait_send()
    lax.fori_loop(1, nz * ny, end_copy, 0)


def on_device(pressure_start, divergence, neighbors, advect_slot, point_cell, point_force):
    n_patch = lax.axis_size("patch")
    nf = lax.axis_size("field")
    ny = math.isqrt(n_patch)
    nz = n_patch // ny
    cells = point_cell.reshape(n_patch, -1)
    if cells.shape[1] < LANES:
        cells = jnp.pad(cells, ((0, 0), (0, LANES - cells.shape[1])), constant_values=-1)

    far = pl.BlockSpec(memory_space=pltpu.HBM)
    dma = pltpu.SemaphoreType.DMA
    slot = (2 * PLANES + 5, 4, LANES)
    inputs = (advect_slot, point_force, pressure_start, divergence, neighbors, cells)
    return pl.pallas_call(
        functools.partial(step_kernel, nz, ny, nf),
        out_shape=jax.ShapeDtypeStruct((n_patch, 3, PLANES, CHUNKS, LANES), jnp.bfloat16),
        in_specs=[far, far, far, far, far, far],
        out_specs=pl.BlockSpec(memory_space=pltpu.VMEM),
        scratch_shapes=[
            pltpu.SMEM((n_patch,), jnp.int32),
            pltpu.VMEM((1, LANES), jnp.float32),
            pltpu.VMEM((n_patch, LANES), jnp.int32),
            pltpu.VMEM((n_patch,) + slot, jnp.bfloat16),
            pltpu.VMEM((2, PLANES + 2, CHUNKS, LANES), jnp.float32),
            pltpu.VMEM((2, PLANES, PPD, AREA), jnp.float32),
            pltpu.SMEM(advect_slot.shape, jnp.int32),
            pltpu.SMEM(point_force.shape, jnp.float32),
            pltpu.VMEM((SLABS, PLANES + 2, PPD, AREA), jnp.float32),
            pltpu.VMEM((SLABS, PLANES + 2, PPD, AREA), jnp.float32),
            pltpu.VMEM((SLABS, PLANES, PPD, AREA), jnp.float32),
            pltpu.VMEM((SLABS, PPD, 6), jnp.int32),
            pltpu.VMEM((nf, 1, LANES), jnp.float32),
            pltpu.VMEM((ny, 1, LANES), jnp.float32),
            pltpu.VMEM((nz, ny, 1, LANES), jnp.float32),
            pltpu.VMEM((nz, ROWS_HOT, ny * LANES), jnp.bfloat16),
            pltpu.VMEM((nz, 256, ny * LANES), jnp.bfloat16),
            pltpu.VMEM((256, ny * LANES), jnp.bfloat16),
            pltpu.VMEM((ROWS_HOT, 256), jnp.float32),
            pltpu.VMEM((SLABS, 5, PPD, LANES), jnp.int32),
            pltpu.VMEM((PPD + 1,) + slot, jnp.float32),
            pltpu.VMEM((n_patch,) + slot, jnp.bfloat16),
            dma((2, PLANES + 1)),
            dma((3, 4)),
            dma((3, 4)),
            dma((nf - 1,)),
            dma((nf - 1,)),
            dma((ny - 1,)),
            dma((ny - 1,)),
            dma((nz - 1,)),
            dma((nz - 1,)),
            dma((n_patch,)),
            dma((n_patch,)),
            dma((2,)),
        ],
        compiler_params=pltpu.CompilerParams(
            collective_id=0, has_side_effects=True, vmem_limit_bytes=48*1024*1024
        ),
        name="step",
    )(*[pltpu.with_memory_space_constraint(v, pltpu.HBM) for v in inputs]).reshape(n_patch, 3, PLANES, AREA)
def solution(mesh):
    in_specs = (
        P("patch", "field", None),
        P("patch", "field", None),
        P("patch", None),
        P("patch"),
        P(),
        P(("patch", "field")),
    )
    out_specs = P("patch", None, "field", None)
    return jax.shard_map(
        on_device, mesh=mesh, in_specs=in_specs, out_specs=out_specs, check_vma=False
    )
```
